32 devices in a mesh: grp: 2 (over y), slab: 8 (over z, x), col: 2 (over core).
Axes of the slice: x: 2, y: 2, z: 4, core: 2. Of those that a mesh axis runs over, the one named last changes fastest.
Arguments:
- states: float32 [4, 64, 128, 1024], P(None, ('grp', 'slab'), 'col'), parts along dimension 1, may hold values from 0 to 1.4, as said below
- cond: float32 [6, 16, 32, 256], P(None, ('grp', 'slab'), 'col'), parts along dimension 1, may hold values from -0.025 to 0.15, as said below
- tension: float32 [32, 64, 512], P(('grp', 'slab'), 'col'), parts along dimension 0, may hold values from 0 to 1
- fiber: int32 [16, 32, 256], P(('grp', 'slab'), 'col'), parts along dimension 0, may hold values from 0 to 63
- disp: float32 [3, 16, 32, 256], P(None, ('grp', 'slab'), 'col'), parts along dimension 1, may hold values from -0.12 to 0.12
Outputs:
- states_next: float32 [4, 64, 128, 1024], P(None, ('grp', 'slab'), 'col'), parts along dimension 1
- tension_next: float32 [32, 64, 512], P(('grp', 'slab'), 'col'), parts along dimension 0
- disp_next: float32 [3, 16, 32, 256], P(None, ('grp', 'slab'), 'col'), parts along dimension 1
- cond_next: float32 [6, 16, 32, 256], P(None, ('grp', 'slab'), 'col'), parts along dimension 1
The draws below stay inside these ranges and needn't reach their ends.
There are 2 independent parts, one for each index of `grp`. The reference program is written for one: setup_inputs(seed, part) draws one part's arguments, and reference() takes and returns one part's arrays. A program takes and returns all parts, laid end to end along the dimension named above; each array names one. Nothing has to cross between parts.
Inputs may be any that keep to these rules, and one draw needn't show every extreme that they name: `states`: component 0 lies in 0 to 1.4, components 1 to 3 in 0 to 1. `cond`: components 0 to 2 lie in 0.05 to 0.15, components 3 to 5 in -0.025 to 0.025.
All inputs are finite; a program needn't handle non-finite values.
Results may differ from the reference program's by a relative error of at most 0.0003.
Values sent between devices are 32-bit elements; how exact they have to be, the bound alone decides.
A program may use at most 192 MiB of HBM per device.

```python
import jax
import jax.numpy as jnp
from jax import lax

NX = 1024
SUB = 4
MECH_STEPS = 2
NFIB = 64
NZ = 32
NY = 128
TZ = 16
TY = 64
TX = 512
MZ = 8
MY = 32
MX = 256


def draw_states(key, part):
    keys = jax.random.split(key, 1)
    rough = jax.random.uniform(keys[0], (4, NZ, NY, NX), jnp.float32)
    scales = jnp.array([1.4, 1.0, 1.0, 1.0], jnp.float32).reshape(4, 1, 1, 1)
    return rough * scales


def draw_cond(key, part):
    keys = jax.random.split(key, 2)
    diagonal = jax.random.uniform(keys[0], (3, MZ, MY, MX), jnp.float32, 0.05, 0.15)
    cross = jax.random.uniform(keys[1], (3, MZ, MY, MX), jnp.float32, -0.025, 0.025)
    return jnp.concatenate([diagonal, cross], 0)


def set_ends(drawn, own_key, least, top_value):
    place = [jax.random.randint(jax.random.fold_in(own_key, axis), (), 0, length) for axis, length in enumerate(drawn.shape)]
    main_axis = drawn.shape.index(max(drawn.shape))
    beside = place[:main_axis] + [(place[main_axis] + 1) % drawn.shape[main_axis]] + place[main_axis + 1:]
    return drawn.at[tuple(place)].set(least).at[tuple(beside)].set(top_value)


def block_levels(own_key, dims, cuts, low, top_value):
    def one(dim, blocks):
        heights = jax.random.uniform(jax.random.fold_in(jax.random.fold_in(own_key, 6), dim), (blocks,), jnp.float32, low / len(cuts), top_value / len(cuts))
        return jnp.repeat(jnp.exp(heights), dims[dim] // blocks).reshape((-1,) + (1,) * (len(dims) - dim - 1))

    level = one(*cuts[0])
    for cut in cuts[1:]:
        level = level * one(*cut)
    return level


def gaussian(stream_key, shape, scale, most, shards=(), kind=jnp.bfloat16):
    drawn = jax.random.normal(stream_key, shape, jnp.float32) * scale
    if len(shards) > 0:
        drawn = block_levels(stream_key, shape, shards, -0.22, 0.18) * drawn
    return jnp.clip(drawn, min=-most, max=most).astype(kind)


def setup_inputs(seed: int = 0, part: int = 0) -> dict:
    key_of = jax.random.split(jax.random.key(seed), 6)
    own_keys = jax.random.split(jax.random.fold_in(key_of[5], part), 6)
    states = draw_states(jax.random.fold_in(jax.random.fold_in(key_of[5], part), 71), part)
    cond = draw_cond(jax.random.fold_in(jax.random.fold_in(key_of[5], part), 71), part)
    tension = jnp.clip(1.0 * jax.random.uniform(own_keys[2], (TZ, TY, TX), jnp.float32) ** block_levels(own_keys[2], (TZ, TY, TX), ((0, 8), (1, 2)), -0.2, 0.2), 0.0, 1.0)
    fiber = set_ends(jax.random.randint(own_keys[3], (MZ, MY, MX), 0, NFIB), jax.random.fold_in(own_keys[3], 1), 0, NFIB - 1).astype(jnp.int32)
    disp = gaussian(own_keys[4], (3, MZ, MY, MX), 0.03, 0.12, ((1, 8), (2, 2)), jnp.float32)
    return dict(states=states, cond=cond, tension=tension, fiber=fiber, disp=disp)


SHARP = 50.0
STEP_TIME = 0.05
LAME_FIRST = 1.0
SHEAR = 0.5
ACTIVE_GAIN = 0.5
MECH_RATE = 0.15
SIGMA_LONG = 0.16
SIGMA_TRANS = 0.04
SMOOTH_WEIGHTS = (0.125, 0.75, 0.125)
SLOPE_WEIGHTS = (-0.5, 0.0, 0.5)
PAIRS = ((0, 0), (1, 1), (2, 2), (0, 1), (0, 2), (1, 2))


def switch(value):
    return 0.5 * (1.0 + jnp.tanh(SHARP * value))


def ionic_rates(volt, gate_v, gate_w, gate_s):
    high_v = switch(volt - 0.3)
    high_w = switch(volt - 0.13)
    high_o = switch(volt - 0.006)
    tau_vminus = (1.0 - high_o) * 60.0 + high_o * 1150.0
    tau_wminus = 60.0 + (15.0 - 60.0) * 0.5 * (1.0 + jnp.tanh(65.0 * (volt - 0.03)))
    tau_soft = 30.0181 + (0.9957 - 30.0181) * 0.5 * (1.0 + jnp.tanh(2.0458 * (volt - 0.65)))
    tau_slow = (1.0 - high_w) * 2.7342 + high_w * 16.0
    tau_open = (1.0 - high_o) * 400.0 + high_o * 6.0
    v_inf = 1.0 - high_o
    w_inf = (1.0 - high_o) * (1.0 - volt / 0.07) + high_o * 0.94
    fast_current = -gate_v * high_v * (volt - 0.3) * (1.55 - volt) / 0.11
    outward = volt * (1.0 - high_w) / tau_open + high_w / tau_soft
    slow_current = -high_w * gate_w * gate_s / 1.8875
    rate_v = (1.0 - high_v) * (v_inf - gate_v) / tau_vminus - high_v * gate_v / 1.4506
    rate_w = (1.0 - high_w) * (w_inf - gate_w) / tau_wminus - high_w * gate_w / 200.0
    rate_s = (0.5 * (1.0 + jnp.tanh(2.0994 * (volt - 0.9087))) - gate_s) / tau_slow
    return -(fast_current + outward + slow_current), rate_v, rate_w, rate_s


def diffusion(padded, coeff):
    centre = padded[1:-1, 1:-1, 1:-1]
    along_z = padded[2:, 1:-1, 1:-1] + padded[:-2, 1:-1, 1:-1] - 2.0 * centre
    along_y = padded[1:-1, 2:, 1:-1] + padded[1:-1, :-2, 1:-1] - 2.0 * centre
    along_x = padded[1:-1, 1:-1, 2:] + padded[1:-1, 1:-1, :-2] - 2.0 * centre
    cross_zy = 0.25 * (padded[2:, 2:, 1:-1] - padded[2:, :-2, 1:-1] - padded[:-2, 2:, 1:-1] + padded[:-2, :-2, 1:-1])
    cross_zx = 0.25 * (padded[2:, 1:-1, 2:] - padded[2:, 1:-1, :-2] - padded[:-2, 1:-1, 2:] + padded[:-2, 1:-1, :-2])
    cross_yx = 0.25 * (padded[1:-1, 2:, 2:] - padded[1:-1, 2:, :-2] - padded[1:-1, :-2, 2:] + padded[1:-1, :-2, :-2])
    return (coeff[0] * along_z + coeff[1] * along_y + coeff[2] * along_x
            + 2.0 * (coeff[3] * cross_zy + coeff[4] * cross_zx + coeff[5] * cross_yx))


def excite_step(padded, volt, gate_v, gate_w, gate_s, coeff):
    ion, rate_v, rate_w, rate_s = ionic_rates(volt, gate_v, gate_w, gate_s)
    new_volt = volt + diffusion(padded, coeff) + STEP_TIME * ion
    return new_volt, gate_v + STEP_TIME * rate_v, gate_w + STEP_TIME * rate_w, gate_s + STEP_TIME * rate_s


def upsample(cond):
    return jnp.repeat(jnp.repeat(jnp.repeat(cond, 4, axis=1), 4, axis=2), 4, axis=3)


def coarsen(field):
    shaped = field.reshape(field.shape[0] // 2, 2, field.shape[1] // 2, 2, field.shape[2] // 2, 2)
    return jnp.mean(shaped, axis=(1, 3, 5))


def fiber_dir(fiber):
    block_index = fiber.astype(jnp.float32)
    theta = -1.0 + 2.0 * block_index / (NFIB - 1)
    tilt = 0.3 * jnp.sin(3.0 * block_index)
    return jnp.stack([jnp.sin(tilt), jnp.cos(tilt) * jnp.sin(theta), jnp.cos(tilt) * jnp.cos(theta)])


def along(field, axis_pos, weights):
    count = field.shape[axis_pos] - 2
    total = weights[0] * lax.slice_in_dim(field, 0, count, axis=axis_pos)
    total = total + weights[1] * lax.slice_in_dim(field, 1, count + 1, axis=axis_pos)
    return total + weights[2] * lax.slice_in_dim(field, 2, count + 2, axis=axis_pos)


def spline_op(padded, direction):
    result = padded
    for dim_pos in range(3):
        result = along(result, dim_pos + 1, SLOPE_WEIGHTS if dim_pos == direction else SMOOTH_WEIGHTS)
    return result


def deformation(padded_disp):
    grads = [spline_op(padded_disp, direction) for direction in range(3)]
    return [[grads[col_pos][row_pos] + (1.0 if row_pos == col_pos else 0.0) for col_pos in range(3)] for row_pos in range(3)]


def first_piola(deform, active, fdir):
    right = [[deform[0][a_pos] * deform[0][b_pos] + deform[1][a_pos] * deform[1][b_pos] + deform[2][a_pos] * deform[2][b_pos]
              for b_pos in range(3)] for a_pos in range(3)]
    strain = [[0.5 * (right[a_pos][b_pos] - (1.0 if a_pos == b_pos else 0.0)) for b_pos in range(3)] for a_pos in range(3)]
    trace_e = strain[0][0] + strain[1][1] + strain[2][2]
    second = []
    for a_pos in range(3):
        row_list = []
        for b_pos in range(3):
            entry = 2.0 * SHEAR * strain[a_pos][b_pos] + ACTIVE_GAIN * active * fdir[a_pos] * fdir[b_pos]
            if a_pos == b_pos:
                entry = LAME_FIRST * trace_e + entry
            row_list.append(entry)
        second.append(row_list)
    pieces = []
    for a_pos in range(3):
        for i_pos in range(3):
            pieces.append(deform[i_pos][0] * second[0][a_pos] + deform[i_pos][1] * second[1][a_pos] + deform[i_pos][2] * second[2][a_pos])
    return jnp.stack(pieces)


def forces(padded_piola):
    total = spline_op(padded_piola[0:3], 0)
    total = total + spline_op(padded_piola[3:6], 1)
    return total + spline_op(padded_piola[6:9], 2)


def metric(deform, fdir):
    det_f = (deform[0][0] * (deform[1][1] * deform[2][2] - deform[1][2] * deform[2][1])
             - deform[0][1] * (deform[1][0] * deform[2][2] - deform[1][2] * deform[2][0])
             + deform[0][2] * (deform[1][0] * deform[2][1] - deform[1][1] * deform[2][0]))
    inverse = [[None, None, None] for row_pos in range(3)]
    for i_pos in range(3):
        for j_pos in range(3):
            cofac = (deform[(i_pos + 1) % 3][(j_pos + 1) % 3] * deform[(i_pos + 2) % 3][(j_pos + 2) % 3]
                     - deform[(i_pos + 1) % 3][(j_pos + 2) % 3] * deform[(i_pos + 2) % 3][(j_pos + 1) % 3])
            inverse[j_pos][i_pos] = cofac / det_f
    along_fiber = [inverse[a_pos][0] * fdir[0] + inverse[a_pos][1] * fdir[1] + inverse[a_pos][2] * fdir[2] for a_pos in range(3)]
    comps = []
    for a_pos, b_pos in PAIRS:
        inv_metric = inverse[a_pos][0] * inverse[b_pos][0] + inverse[a_pos][1] * inverse[b_pos][1] + inverse[a_pos][2] * inverse[b_pos][2]
        comps.append(SIGMA_TRANS * inv_metric + (SIGMA_LONG - SIGMA_TRANS) * along_fiber[a_pos] * along_fiber[b_pos])
    return jnp.stack(comps)


def mechanics(disp, active, fdir, extend):
    for turn_index in range(MECH_STEPS):
        deform = deformation(extend(disp))
        piola = first_piola(deform, active, fdir)
        disp = disp + MECH_RATE * forces(extend(piola))
    deform = deformation(extend(disp))
    return disp, metric(deform, fdir)


def pad_space(field):
    return jnp.pad(field, ((0, 0), (1, 1), (1, 1), (1, 1)))


def reference(states, cond, tension, fiber, disp):
    volt, gate_v, gate_w, gate_s = states[0], states[1], states[2], states[3]
    coeff = upsample(cond)
    for turn_index in range(SUB):
        padded = jnp.pad(volt, 1)
        volt, gate_v, gate_w, gate_s = excite_step(padded, volt, gate_v, gate_w, gate_s, coeff)
    states_next = jnp.stack([volt, gate_v, gate_w, gate_s])
    tension_next = tension + 0.5 * (coarsen(volt) - tension)
    active = coarsen(tension_next)
    fdir = fiber_dir(fiber)
    disp_next, cond_next = mechanics(disp, active, fdir, pad_space)
    return states_next, tension_next, disp_next, cond_next
```

```python
import functools

import jax
import jax.numpy as jnp
from jax import lax
from jax.experimental import pallas as pl
from jax.experimental.pallas import tpu as pltpu
from jax.sharding import PartitionSpec as P

SUB = 4
MECH_STEPS = 2
NFIB = 64
STEP_TIME = 0.05
MECH_RATE = 0.15
SIGMA_LONG = 0.16
SIGMA_TRANS = 0.04
PAIRS = ((0, 0), (1, 1), (2, 2), (0, 1), (0, 2), (1, 2))
MESH = pl.DeviceIdType.MESH
HI = lax.Precision.HIGHEST
F32 = jnp.float32
TILE = 8
CHUNK = 256


def ionic(u, v, w, s):
    th_v = jnp.tanh(50.0 * (u - 0.3))
    th_w = jnp.tanh(50.0 * (u - 0.13))
    th_o = jnp.tanh(50.0 * (u - 0.006))
    th_m = jnp.tanh(65.0 * (u - 0.03))
    th_s = jnp.tanh(2.0458 * (u - 0.65))
    th_r = jnp.tanh(2.0994 * (u - 0.9087))
    hv = 0.5 + 0.5 * th_v
    hw = 0.5 + 0.5 * th_w
    ho = 0.5 + 0.5 * th_o
    nv = 1.0 - hv
    nw = 1.0 - hw
    no = 1.0 - ho
    tau_v = 605.0 + 545.0 * th_o
    tau_w = 37.5 - 22.5 * th_m
    tau_so = 15.5069 - 14.5112 * th_s
    tau_s = 9.3671 + 6.6329 * th_w
    tau_o = 203.0 - 197.0 * th_o
    w_inf = no * (1.0 - u * (1.0 / 0.07)) + 0.94 * ho
    fast = v * hv * (u - 0.3) * (1.55 - u) * (STEP_TIME / 0.11)
    slow = hw * (w * s) * (STEP_TIME / 1.8875)
    out = (u * nw * tau_so + hw * tau_o) * (STEP_TIME / (tau_o * tau_so))
    du = fast - out + slow
    inv = STEP_TIME / (tau_v * tau_w)
    v2 = v + nv * (no - v) * (tau_w * inv) - hv * v * (STEP_TIME / 1.4506)
    w2 = w + nw * (w_inf - w) * (tau_v * inv) - hw * w * (STEP_TIME / 200.0)
    s2 = s + (0.5 + 0.5 * th_r - s) * (STEP_TIME / tau_s)
    return du, v2, w2, s2


def iota2(shape, dim):
    return lax.broadcasted_iota(jnp.int32, shape, dim)


def excite_kernel(
    slabs, states, cond, tension, out, ten_out, act_out,
    ubuf, coeff, dif, load_sem, sz, rz, sc, rc, sy, ry,
):
    grp = lax.axis_index("grp")
    slab = lax.axis_index("slab")
    col = lax.axis_index("col")
    other = 1 - col
    depth, rows, width = out.shape[1:]
    tiles = rows // TILE
    has_up = slab < slabs - 1
    has_dn = slab > 0
    edge_src = rows - (rows - TILE) * col
    edge_dst = (rows + TILE) * col

    load_u = pltpu.make_async_copy(
        states.at[0], ubuf.at[0, pl.ds(1, depth), pl.ds(TILE, rows), :], load_sem.at[0]
    )
    load_g = pltpu.make_async_copy(
        states.at[pl.ds(1, 3)], out.at[pl.ds(1, 3)], load_sem.at[1]
    )
    load_u.start()
    load_g.start()

    barrier = pltpu.get_barrier_semaphore()

    def greet(where):
        pl.semaphore_signal(barrier, inc=1, device_id=where, device_id_type=MESH)

    greet((grp, slab, other))

    @pl.when(has_up)
    def _():
        greet((grp, slab + 1, col))
        greet((grp, slab + 1, other))

    @pl.when(has_dn)
    def _():
        greet((grp, slab - 1, col))
        greet((grp, slab - 1, other))

    blank = jnp.zeros((TILE, width), F32)

    def clear_y(n, c):
        ubuf[n // (depth + 2), n % (depth + 2), pl.ds(pl.multiple_of(edge_dst, TILE), TILE), :] = blank
        return c

    lax.fori_loop(0, SUB * (depth + 2), clear_y, 0)

    def clear_z(layer):
        per = rows // TILE + 2

        def body(n, c):
            ubuf[n // per, layer, pl.ds(pl.multiple_of((n % per) * TILE, TILE), TILE), :] = blank
            return c

        lax.fori_loop(0, SUB * per, body, 0)

    @pl.when(slab == 0)
    def _():
        clear_z(0)

    @pl.when(slab == slabs - 1)
    def _():
        clear_z(depth + 1)

    spread_x = (iota2((128, 512), 0) == iota2((128, 512), 1) // 4).astype(F32)
    spread_y = (iota2((rows, rows // 4), 0) // 4 == iota2((rows, rows // 4), 1)).astype(F32)
    for c in range(6):
        for h in range(width // 512):
            part = jnp.dot(
                cond[c, 0, :, h * 128 : (h + 1) * 128], spread_x, precision=HI,
                preferred_element_type=F32,
            )
            part = jnp.dot(spread_y, part, precision=HI, preferred_element_type=F32)
            coeff[c, :, h * 512 : (h + 1) * 512] = part if c < 3 else 0.5 * part

    def row_of(step):
        return jnp.where(col == 1, step, tiles - 1 - step)

    def copy_z(slot, way, step):
        at = pl.ds(pl.multiple_of(TILE + TILE * row_of(step), TILE), TILE)
        src = depth if way == 0 else 1
        dst = 0 if way == 0 else depth + 1
        to = slab + 1 if way == 0 else slab - 1
        return pltpu.make_async_remote_copy(
            src_ref=ubuf.at[slot, src, at, :],
            dst_ref=ubuf.at[slot, dst, at, :],
            send_sem=sz.at[slot, way, step],
            recv_sem=rz.at[slot, way, step],
            device_id=(grp, to, col),
            device_id_type=MESH,
        )

    def copy_c(slot, way):
        src = depth if way == 0 else 1
        dst = 0 if way == 0 else depth + 1
        to = slab + 1 if way == 0 else slab - 1
        return pltpu.make_async_remote_copy(
            src_ref=ubuf.at[slot, src, pl.ds(pl.multiple_of(edge_src, TILE), TILE), :],
            dst_ref=ubuf.at[slot, dst, pl.ds(pl.multiple_of(edge_dst, TILE), TILE), :],
            send_sem=sc.at[slot, way],
            recv_sem=rc.at[slot, way],
            device_id=(grp, to, other),
            device_id_type=MESH,
        )

    def copy_y(slot):
        return pltpu.make_async_remote_copy(
            src_ref=ubuf.at[slot, pl.ds(1, depth), pl.ds(pl.multiple_of(edge_src, TILE), TILE), :],
            dst_ref=ubuf.at[slot, pl.ds(1, depth), pl.ds(pl.multiple_of(edge_dst, TILE), TILE), :],
            send_sem=sy.at[slot],
            recv_sem=ry.at[slot],
            device_id=(grp, slab, other),
            device_id_type=MESH,
        )

    def both(do_up, do_dn):
        pl.when(has_up)(do_up)
        pl.when(has_dn)(do_dn)

    def send_z(slot, step):
        both(lambda: copy_z(slot, 0, step).start(), lambda: copy_z(slot, 1, step).start())

    def send_c(slot):
        both(lambda: copy_c(slot, 0).start(), lambda: copy_c(slot, 1).start())

    def recv_z(slot, step):
        both(lambda: copy_z(slot, 1, step).wait_recv(), lambda: copy_z(slot, 0, step).wait_recv())

    def recv_c(slot):
        both(lambda: copy_c(slot, 1).wait_recv(), lambda: copy_c(slot, 0).wait_recv())

    peers = 1 + 2 * has_up.astype(jnp.int32) + 2 * has_dn.astype(jnp.int32)
    pl.semaphore_wait(barrier, peers)

    load_u.wait()
    send_z(0, 0)
    send_c(0)
    copy_y(0).start()

    def initial(step, c):
        send_z(0, step)
        return c

    lax.fori_loop(1, tiles, initial, 0)
    load_g.wait()

    lane = iota2((TILE, width), 1)

    def left(f):
        return jnp.where(lane == 0, 0.0, pltpu.roll(f, 1, 1))

    def right(f):
        return jnp.where(lane == width - 1, 0.0, pltpu.roll(f, width - 1, 1))

    def layer(k, z, r):
        base = pl.multiple_of(TILE * r, TILE)
        here = pl.ds(base, TILE)
        tall = pl.ds(base, 3 * TILE)
        below = ubuf[k, z, tall, :]
        mid = ubuf[k, z + 1, tall, :]
        above = ubuf[k, z + 2, tall, :]
        odd = above - below
        centre = mid[TILE : 2 * TILE]
        odd0 = odd[TILE : 2 * TILE]
        north = mid[TILE + 1 : 2 * TILE + 1]
        south = mid[TILE - 1 : 2 * TILE - 1]
        slope = north - south
        twice = 2.0 * centre
        total = coeff[0, here, :] * (
            above[TILE : 2 * TILE] + below[TILE : 2 * TILE] - twice
        )
        total = total + coeff[1, here, :] * (north + south - twice)
        total = total + coeff[2, here, :] * (right(centre) + left(centre) - twice)
        total = total + coeff[3, here, :] * (
            odd[TILE + 1 : 2 * TILE + 1] - odd[TILE - 1 : 2 * TILE - 1]
        )
        total = total + coeff[4, here, :] * (right(odd0) - left(odd0))
        total = total + coeff[5, here, :] * (right(slope) - left(slope))
        dif[...] = total + centre
        up = pl.ds(pl.multiple_of(base + TILE, TILE), TILE)
        for x in range(0, width, CHUNK):
            xs = pl.ds(x, CHUNK)
            du, v2, w2, s2 = ionic(
                ubuf[k, z + 1, up, xs], out[1, z, here, xs], out[2, z, here, xs],
                out[3, z, here, xs],
            )
            u2 = dif[:, xs] + du
            ubuf[k + 1, z + 1, up, xs] = u2
            out[0, z, here, xs] = u2
            out[1, z, here, xs] = v2
            out[2, z, here, xs] = w2
            out[3, z, here, xs] = s2

    def chunk(n, c):
        k = n // tiles
        step = n % tiles
        r = row_of(step)

        @pl.when(step == 0)
        def _():
            recv_z(k, 0)
            copy_y(k).wait_recv()
            recv_c(k)

        @pl.when(step < tiles - 1)
        def _():
            recv_z(k, step + 1)

        def outer(m, c):
            layer(k, m * (depth - 1), r)
            return c

        lax.fori_loop(0, 2, outer, 0)

        @pl.when(k < SUB - 1)
        def _():
            send_z(k + 1, step)

            @pl.when(step == 0)
            def _():
                send_c(k + 1)

        def inner(m, c):
            layer(k, m, r)
            return c

        lax.fori_loop(1, depth - 1, inner, 0)

        @pl.when((k < SUB - 1) & (step == 0))
        def _():
            copy_y(k + 1).start()

        return c

    lax.fori_loop(0, SUB * tiles, chunk, 0)

    pair_x = (iota2((256, 128), 0) // 2 == iota2((256, 128), 1)).astype(F32)
    half = rows // 2
    pair_y = (iota2((half, rows), 0) == iota2((half, rows), 1) // 2).astype(F32)
    pair_y2 = (iota2((half // 2, half), 0) == iota2((half // 2, half), 1) // 2).astype(F32)
    for h in range(width // 256):
        for q in range(depth // 2):
            xs = slice(h * 256, (h + 1) * 256)
            layers = out[0, 2 * q, :, xs] + out[0, 2 * q + 1, :, xs]
            mean = jnp.dot(layers, pair_x, precision=HI, preferred_element_type=F32)
            mean = 0.125 * jnp.dot(pair_y, mean, precision=HI, preferred_element_type=F32)
            xo = slice(h * 128, (h + 1) * 128)
            before = tension[q, :, xo]
            ten_out[q, :, xo] = before + 0.5 * (mean - before)
    for h in range(width // 512):
        xs = slice(h * 256, (h + 1) * 256)
        layers = ten_out[0, :, xs] + ten_out[1, :, xs]
        mean = jnp.dot(layers, pair_x, precision=HI, preferred_element_type=F32)
        mean = 0.125 * jnp.dot(pair_y2, mean, precision=HI, preferred_element_type=F32)
        act_out[0, :, h * 128 : (h + 1) * 128] = mean

    copy_y(0).wait_send()

    def drain(slot, c):
        both(lambda: copy_c(slot, 0).wait_send(), lambda: copy_c(slot, 1).wait_send())

        @pl.when(slot > 0)
        def _():
            copy_y(slot).wait_send()

        def tile(step, c):
            both(
                lambda: copy_z(slot, 0, step).wait_send(),
                lambda: copy_z(slot, 1, step).wait_send(),
            )
            return c

        return lax.fori_loop(0, tiles, tile, c)

    lax.fori_loop(0, SUB, drain, 0)


def excite(slabs, states, cond, tension):
    _, depth, rows, width = states.shape
    tiles = rows // TILE
    vmem = pl.BlockSpec(memory_space=pltpu.VMEM)
    dma = pltpu.SemaphoreType.DMA
    return pl.pallas_call(
        functools.partial(excite_kernel, slabs),
        out_shape=(
            jax.ShapeDtypeStruct(states.shape, F32),
            jax.ShapeDtypeStruct(tension.shape, F32),
            jax.ShapeDtypeStruct(cond.shape[1:], F32),
        ),
        in_specs=[pl.BlockSpec(memory_space=pl.ANY), vmem, vmem],
        out_specs=(vmem, vmem, vmem),
        scratch_shapes=[
            pltpu.VMEM((SUB + 1, depth + 2, rows + 2 * TILE, width), F32),
            pltpu.VMEM((6, rows, width), F32),
            pltpu.VMEM((TILE, width), F32),
            dma((2,)),
            dma((SUB, 2, tiles)),
            dma((SUB, 2, tiles)),
            dma((SUB, 2)),
            dma((SUB, 2)),
            dma((SUB,)),
            dma((SUB,)),
        ],
        compiler_params=pltpu.CompilerParams(
            collective_id=0, has_side_effects=True, vmem_limit_bytes=40 << 20
        ),
        cost_estimate=pl.CostEstimate(
            flops=200_000_000, bytes_accessed=16 << 20, transcendentals=6_000_000
        ),
        name="excite",
    )(states, cond, tension)


def first_piola(f, active, fdir):
    second = {}
    for a in range(3):
        for b in range(a, 3):
            right = f[0][a] * f[0][b] + f[1][a] * f[1][b] + f[2][a] * f[2][b]
            second[a, b] = 0.5 * (right - (1.0 if a == b else 0.0))
    trace = second[0, 0] + second[1, 1] + second[2, 2]
    pull = 0.5 * active
    for a in range(3):
        scaled = pull * fdir[a]
        for b in range(a, 3):
            second[a, b] = second[a, b] + scaled * fdir[b]
        second[a, a] = second[a, a] + trace
    for a in range(3):
        for b in range(a):
            second[a, b] = second[b, a]
    return [
        f[i][0] * second[0, a] + f[i][1] * second[1, a] + f[i][2] * second[2, a]
        for a in range(3)
        for i in range(3)
    ]


def metric(f, fdir):
    cof = [[None] * 3 for _ in range(3)]
    for i in range(3):
        for j in range(3):
            cof[i][j] = (
                f[(i + 1) % 3][(j + 1) % 3] * f[(i + 2) % 3][(j + 2) % 3]
                - f[(i + 1) % 3][(j + 2) % 3] * f[(i + 2) % 3][(j + 1) % 3]
            )
    det = f[0][0] * cof[0][0] + f[0][1] * cof[0][1] + f[0][2] * cof[0][2]
    scale = 1.0 / det
    inverse = [[cof[i][j] * scale for i in range(3)] for j in range(3)]
    g = [inverse[a][0] * fdir[0] + inverse[a][1] * fdir[1] + inverse[a][2] * fdir[2] for a in range(3)]
    comps = []
    for a, b in PAIRS:
        inner = (
            inverse[a][0] * inverse[b][0]
            + inverse[a][1] * inverse[b][1]
            + inverse[a][2] * inverse[b][2]
        )
        comps.append(SIGMA_TRANS * inner + (SIGMA_LONG - SIGMA_TRANS) * (g[a] * g[b]))
    return comps


RADIUS = 2 * MECH_STEPS + 1


def mech_kernel(slabs, where, fixed, active, disp_out, cond_out, win, stress):
    slab = where[0]
    rows, width = active.shape[2], active.shape[3]
    lane = iota2((rows, width), 1)
    line = iota2((rows, width), 0)

    def left(f):
        return jnp.where(lane == 0, 0.0, pltpu.roll(f, 1, 1))

    def right(f):
        return jnp.where(lane == width - 1, 0.0, pltpu.roll(f, width - 1, 1))

    def south(f):
        return jnp.where(line == 0, 0.0, pltpu.roll(f, 1, 0))

    def north(f):
        return jnp.where(line == rows - 1, 0.0, pltpu.roll(f, rows - 1, 0))

    def sx(f):
        return 0.125 * (left(f) + right(f)) + 0.75 * f

    def dx(f):
        return 0.5 * (right(f) - left(f))

    def sy(f):
        return 0.125 * (south(f) + north(f)) + 0.75 * f

    def dy(f):
        return 0.5 * (north(f) - south(f))

    def inside(j):
        zz = slab + j - RADIUS
        return (zz >= 0) & (zz < slabs), jnp.clip(zz, 0, slabs - 1)

    def fill(j, c):
        ok, zz = inside(j)
        for i in range(3):
            win[i, j] = jnp.where(ok, fixed[i, zz], 0.0)
        return c

    lax.fori_loop(0, 2 * RADIUS + 1, fill, 0)

    def deformation(j):
        f = []
        for i in range(3):
            low, mid, high = win[i, j - 1], win[i, j], win[i, j + 1]
            zs = 0.125 * (low + high) + 0.75 * mid
            zd = 0.5 * (high - low)
            f.append([sy(sx(zd)), dy(sx(zs)), sy(dx(zs))])
            f[i][i] = f[i][i] + 1.0
        return f

    def directions(zz):
        return [fixed[3 + a, zz] for a in range(3)]

    def stresses(j, c):
        ok, zz = inside(j)
        pieces = first_piola(deformation(j), active[0, zz], directions(zz))
        for n in range(9):
            stress[n, j] = jnp.where(ok, pieces[n], 0.0)
        return c

    def move(j, c):
        ok, _ = inside(j)
        for i in range(3):
            zd = 0.5 * (stress[i, j + 1] - stress[i, j - 1])
            ys = 0.125 * (stress[3 + i, j - 1] + stress[3 + i, j + 1]) + 0.75 * stress[3 + i, j]
            xs = 0.125 * (stress[6 + i, j - 1] + stress[6 + i, j + 1]) + 0.75 * stress[6 + i, j]
            force = sy(sx(zd) + dx(xs)) + dy(sx(ys))
            win[i, j] = jnp.where(ok, win[i, j] + MECH_RATE * force, 0.0)
        return c

    for turn in range(MECH_STEPS):
        reach = RADIUS - 1 - 2 * turn
        lax.fori_loop(RADIUS - reach, RADIUS + reach + 1, stresses, 0)
        reach = reach - 1
        lax.fori_loop(RADIUS - reach, RADIUS + reach + 1, move, 0)

    comps = metric(deformation(RADIUS), directions(slab))
    half = disp_out.shape[2]
    first = where[1] == 0
    for i in range(3):
        whole = win[i, RADIUS]
        disp_out[i, 0] = jnp.where(first, whole[:half], whole[half:])
    for n in range(6):
        cond_out[n, 0] = jnp.where(first, comps[n][:half], comps[n][half:])


def mechanics(slabs, where, fixed, active, rows):
    width = active.shape[3]
    full = active.shape[2]
    vmem = pl.BlockSpec(memory_space=pltpu.VMEM)
    return pl.pallas_call(
        functools.partial(mech_kernel, slabs),
        out_shape=(
            jax.ShapeDtypeStruct((3, 1, rows, width), F32),
            jax.ShapeDtypeStruct((6, 1, rows, width), F32),
        ),
        in_specs=[pl.BlockSpec(memory_space=pltpu.SMEM), vmem, vmem],
        out_specs=(vmem, vmem),
        scratch_shapes=[
            pltpu.VMEM((3, 2 * RADIUS + 1, full, width), F32),
            pltpu.VMEM((9, 2 * RADIUS + 1, full, width), F32),
        ],
        compiler_params=pltpu.CompilerParams(vmem_limit_bytes=40 << 20),
        name="mechanics",
    )(where, fixed, active)


def fiber_dir(fiber):
    index = fiber.astype(F32)
    theta = -1.0 + 2.0 * index / (NFIB - 1)
    tilt = 0.3 * jnp.sin(3.0 * index)
    return jnp.stack(
        [jnp.sin(tilt), jnp.cos(tilt) * jnp.sin(theta), jnp.cos(tilt) * jnp.cos(theta)]
    )


def gathered(field):
    whole = lax.all_gather(field, ("slab", "col"))
    slabs, cols = lax.axis_size("slab"), lax.axis_size("col")
    count, _, rows, width = field.shape
    whole = whole.reshape(slabs, cols, count, rows, width)
    return whole.transpose(2, 0, 1, 3, 4).reshape(count, slabs, cols * rows, width)


def on_device(slabs, states, cond, tension, fiber, disp):
    fixed = gathered(jnp.concatenate([disp, fiber_dir(fiber)]))
    states_next, tension_next, active = excite(slabs, states, cond, tension)
    whole = gathered(active[None])
    where = jnp.stack([lax.axis_index("slab"), lax.axis_index("col")]).astype(jnp.int32)
    disp_next, cond_next = mechanics(slabs, where, fixed, whole, disp.shape[2])
    return states_next, tension_next, disp_next, cond_next


def solution(mesh):
    wide = P(None, ("grp", "slab"), "col", None)
    flat = P(("grp", "slab"), "col", None)
    return jax.shard_map(
        functools.partial(on_device, mesh.shape["slab"]),
        mesh=mesh,
        in_specs=(wide, wide, flat, flat, wide),
        out_specs=(wide, flat, wide, wide),
        check_vma=False,
    )
```

```python
import functools

import jax
import jax.numpy as jnp
from jax import lax
from jax.experimental import pallas as pl
from jax.experimental.pallas import tpu as pltpu
from jax.sharding import PartitionSpec as P

SUB = 4
MECH_STEPS = 2
NFIB = 64
STEP_TIME = 0.05
MECH_RATE = 0.15
SIGMA_LONG = 0.16
SIGMA_TRANS = 0.04
PAIRS = ((0, 0), (1, 1), (2, 2), (0, 1), (0, 2), (1, 2))
MESH = pl.DeviceIdType.MESH
HI = lax.Precision.HIGHEST
F32 = jnp.float32
TILE = 8
CHUNK = 256
RADIUS = 2 * MECH_STEPS + 1
REACH = RADIUS - 1


def ionic(u, v, w, s):
    th_v = jnp.tanh(50.0 * (u - 0.3))
    th_w = jnp.tanh(50.0 * (u - 0.13))
    th_o = jnp.tanh(50.0 * (u - 0.006))
    th_m = jnp.tanh(65.0 * (u - 0.03))
    th_s = jnp.tanh(2.0458 * (u - 0.65))
    th_r = jnp.tanh(2.0994 * (u - 0.9087))
    hv = 0.5 + 0.5 * th_v
    hw = 0.5 + 0.5 * th_w
    ho = 0.5 + 0.5 * th_o
    nv = 1.0 - hv
    nw = 1.0 - hw
    no = 1.0 - ho
    tau_v = 605.0 + 545.0 * th_o
    tau_w = 37.5 - 22.5 * th_m
    tau_so = 15.5069 - 14.5112 * th_s
    tau_s = 9.3671 + 6.6329 * th_w
    tau_o = 203.0 - 197.0 * th_o
    w_inf = no * (1.0 - u * (1.0 / 0.07)) + 0.94 * ho
    fast = v * hv * (u - 0.3) * (1.55 - u) * (STEP_TIME / 0.11)
    slow = hw * (w * s) * (STEP_TIME / 1.8875)
    out = (u * nw * tau_so + hw * tau_o) * (STEP_TIME / (tau_o * tau_so))
    du = fast - out + slow
    inv = STEP_TIME / (tau_v * tau_w)
    v2 = v + nv * (no - v) * (tau_w * inv) - hv * v * (STEP_TIME / 1.4506)
    w2 = w + nw * (w_inf - w) * (tau_v * inv) - hw * w * (STEP_TIME / 200.0)
    s2 = s + (0.5 + 0.5 * th_r - s) * (STEP_TIME / tau_s)
    return du, v2, w2, s2


def iota2(shape, dim):
    return lax.broadcasted_iota(jnp.int32, shape, dim)


def excite_kernel(
    slabs, states, cond_hbm, ten_hbm, out_hbm, ten_out, act_out,
    ubuf, out, cond, tension, coeff, dif, act_win,
    load_sem, store_sem, sz, rz, sc, rc, sy, ry, sa, ra,
):
    grp = lax.axis_index("grp")
    slab = lax.axis_index("slab")
    col = lax.axis_index("col")
    other = 1 - col
    depth, rows, width = out.shape[1:]
    tiles = rows // TILE
    has_up = slab < slabs - 1
    has_dn = slab > 0
    edge_src = rows - (rows - TILE) * col
    edge_dst = (rows + TILE) * col

    load_u = pltpu.make_async_copy(
        states.at[0], ubuf.at[0, pl.ds(1, depth), pl.ds(TILE, rows), :], load_sem.at[0]
    )
    load_g = pltpu.make_async_copy(
        states.at[pl.ds(1, 3)], out.at[pl.ds(1, 3)], load_sem.at[1]
    )
    load_c = pltpu.make_async_copy(cond_hbm, cond, load_sem.at[2])
    load_t = pltpu.make_async_copy(ten_hbm, tension, load_sem.at[3])
    load_u.start()
    load_c.start()
    load_g.start()
    load_t.start()

    barrier = pltpu.get_barrier_semaphore()

    def greet(where):
        pl.semaphore_signal(barrier, inc=1, device_id=where, device_id_type=MESH)

    peers = -1
    for d in range(-REACH, REACH + 1):
        valid = (slab + d >= 0) & (slab + d < slabs)
        peers = peers + 2 * valid.astype(jnp.int32)

        @pl.when(valid)
        def _(d=d):
            greet((grp, slab + d, other))
            if d != 0:
                greet((grp, slab + d, col))

        @pl.when(jnp.logical_not(valid))
        def _(d=d):
            act_win[d + REACH] = jnp.zeros(act_win.shape[1:], F32)

    blank = jnp.zeros((TILE, width), F32)

    def clear_y(n, c):
        ubuf[n // (depth + 2), n % (depth + 2), pl.ds(pl.multiple_of(edge_dst, TILE), TILE), :] = blank
        return c

    lax.fori_loop(0, SUB * (depth + 2), clear_y, 0)

    def clear_z(layer):
        per = rows // TILE + 2

        def body(n, c):
            ubuf[n // per, layer, pl.ds(pl.multiple_of((n % per) * TILE, TILE), TILE), :] = blank
            return c

        lax.fori_loop(0, SUB * per, body, 0)

    @pl.when(slab == 0)
    def _():
        clear_z(0)

    @pl.when(slab == slabs - 1)
    def _():
        clear_z(depth + 1)

    def row_of(step):
        return jnp.where(col == 1, step, tiles - 1 - step)

    def copy_z(slot, way, step):
        at = pl.ds(pl.multiple_of(TILE + TILE * row_of(step), TILE), TILE)
        src = depth if way == 0 else 1
        dst = 0 if way == 0 else depth + 1
        to = slab + 1 if way == 0 else slab - 1
        return pltpu.make_async_remote_copy(
            src_ref=ubuf.at[slot, src, at, :],
            dst_ref=ubuf.at[slot, dst, at, :],
            send_sem=sz.at[slot, way, step],
            recv_sem=rz.at[slot, way, step],
            device_id=(grp, to, col),
            device_id_type=MESH,
        )

    def copy_c(slot, way):
        at = depth + 1 if way == 0 else 0
        return pltpu.make_async_remote_copy(
            src_ref=ubuf.at[slot, at, pl.ds(pl.multiple_of(edge_src, TILE), TILE), :],
            dst_ref=ubuf.at[slot, at, pl.ds(pl.multiple_of(edge_dst, TILE), TILE), :],
            send_sem=sc.at[slot, way],
            recv_sem=rc.at[slot, way],
            device_id=(grp, slab, other),
            device_id_type=MESH,
        )

    def copy_y(slot):
        return pltpu.make_async_remote_copy(
            src_ref=ubuf.at[slot, pl.ds(1, depth), pl.ds(pl.multiple_of(edge_src, TILE), TILE), :],
            dst_ref=ubuf.at[slot, pl.ds(1, depth), pl.ds(pl.multiple_of(edge_dst, TILE), TILE), :],
            send_sem=sy.at[slot],
            recv_sem=ry.at[slot],
            device_id=(grp, slab, other),
            device_id_type=MESH,
        )

    def both(do_up, do_dn):
        pl.when(has_up)(do_up)
        pl.when(has_dn)(do_dn)

    def send_z(slot, step):
        both(lambda: copy_z(slot, 0, step).start(), lambda: copy_z(slot, 1, step).start())

    def send_c(slot):
        both(lambda: copy_c(slot, 0).start(), lambda: copy_c(slot, 1).start())

    def recv_z(slot, step):
        both(lambda: copy_z(slot, 1, step).wait_recv(), lambda: copy_z(slot, 0, step).wait_recv())

    def recv_c(slot):
        both(lambda: copy_c(slot, 0).wait_recv(), lambda: copy_c(slot, 1).wait_recv())

    pl.semaphore_wait(barrier, peers)

    load_u.wait()
    send_z(0, 0)
    copy_y(0).start()

    def initial(step, c):
        send_z(0, step)
        return c

    lax.fori_loop(1, tiles, initial, 0)
    load_c.wait()

    spread_x = (iota2((128, 512), 0) == iota2((128, 512), 1) // 4).astype(F32)
    spread_y = (iota2((rows, rows // 4), 0) // 4 == iota2((rows, rows // 4), 1)).astype(F32)
    for c in range(6):
        for h in range(width // 512):
            part = jnp.dot(
                cond[c, 0, :, h * 128 : (h + 1) * 128], spread_x, precision=HI,
                preferred_element_type=F32,
            )
            part = jnp.dot(spread_y, part, precision=HI, preferred_element_type=F32)
            coeff[c, :, h * 512 : (h + 1) * 512] = part if c < 3 else 0.5 * part

    load_g.wait()

    lane = iota2((TILE, width), 1)

    def left(f):
        return jnp.where(lane == 0, 0.0, pltpu.roll(f, 1, 1))

    def right(f):
        return jnp.where(lane == width - 1, 0.0, pltpu.roll(f, width - 1, 1))

    def layer(k, z, r):
        base = pl.multiple_of(TILE * r, TILE)
        here = pl.ds(base, TILE)
        tall = pl.ds(base, 3 * TILE)
        below = ubuf[k, z, tall, :]
        mid = ubuf[k, z + 1, tall, :]
        above = ubuf[k, z + 2, tall, :]
        odd = above - below
        centre = mid[TILE : 2 * TILE]
        odd0 = odd[TILE : 2 * TILE]
        north = mid[TILE + 1 : 2 * TILE + 1]
        south = mid[TILE - 1 : 2 * TILE - 1]
        slope = north - south
        twice = 2.0 * centre
        total = coeff[0, here, :] * (
            above[TILE : 2 * TILE] + below[TILE : 2 * TILE] - twice
        )
        total = total + coeff[1, here, :] * (north + south - twice)
        total = total + coeff[2, here, :] * (right(centre) + left(centre) - twice)
        total = total + coeff[3, here, :] * (
            odd[TILE + 1 : 2 * TILE + 1] - odd[TILE - 1 : 2 * TILE - 1]
        )
        total = total + coeff[4, here, :] * (right(odd0) - left(odd0))
        total = total + coeff[5, here, :] * (right(slope) - left(slope))
        dif[...] = total + centre
        up = pl.ds(pl.multiple_of(base + TILE, TILE), TILE)
        for x in range(0, width, CHUNK):
            xs = pl.ds(x, CHUNK)
            du, v2, w2, s2 = ionic(
                ubuf[k, z + 1, up, xs], out[1, z, here, xs], out[2, z, here, xs],
                out[3, z, here, xs],
            )
            u2 = dif[:, xs] + du
            ubuf[k + 1, z + 1, up, xs] = u2
            out[0, z, here, xs] = u2
            out[1, z, here, xs] = v2
            out[2, z, here, xs] = w2
            out[3, z, here, xs] = s2

    def leave(step):
        at = pl.ds(pl.multiple_of(TILE * row_of(step), TILE), TILE)
        return pltpu.make_async_copy(
            out.at[:, :, at, :], out_hbm.at[:, :, at, :], store_sem.at[step]
        )

    def chunk(n, c):
        k = n // tiles
        step = n % tiles
        r = row_of(step)

        @pl.when(step == 0)
        def _():
            recv_z(k, 0)
            send_c(k)

        @pl.when(step < tiles - 1)
        def _():
            recv_z(k, step + 1)

        @pl.when(step == 0)
        def _():
            copy_y(k).wait_recv()
            recv_c(k)

        def outer(m, c):
            layer(k, m * (depth - 1), r)
            return c

        lax.fori_loop(0, 2, outer, 0)

        @pl.when(k < SUB - 1)
        def _():
            send_z(k + 1, step)

        def inner(m, c):
            layer(k, m, r)
            return c

        lax.fori_loop(1, depth - 1, inner, 0)

        @pl.when((k < SUB - 1) & (step == 0))
        def _():
            copy_y(k + 1).start()

        @pl.when(k == SUB - 1)
        def _():
            leave(step).start()

        return c

    lax.fori_loop(0, SUB * tiles, chunk, 0)

    load_t.wait()

    pair_x = (iota2((256, 128), 0) // 2 == iota2((256, 128), 1)).astype(F32)
    half = rows // 2
    pair_y = (iota2((half, rows), 0) == iota2((half, rows), 1) // 2).astype(F32)
    pair_y2 = (iota2((half // 2, half), 0) == iota2((half // 2, half), 1) // 2).astype(F32)
    for h in range(width // 256):
        for q in range(depth // 2):
            xs = slice(h * 256, (h + 1) * 256)
            layers = out[0, 2 * q, :, xs] + out[0, 2 * q + 1, :, xs]
            mean = jnp.dot(layers, pair_x, precision=HI, preferred_element_type=F32)
            mean = 0.125 * jnp.dot(pair_y, mean, precision=HI, preferred_element_type=F32)
            xo = slice(h * 128, (h + 1) * 128)
            before = tension[q, :, xo]
            ten_out[q, :, xo] = before + 0.5 * (mean - before)
    for h in range(width // 512):
        xs = slice(h * 256, (h + 1) * 256)
        layers = ten_out[0, :, xs] + ten_out[1, :, xs]
        mean = jnp.dot(layers, pair_x, precision=HI, preferred_element_type=F32)
        mean = 0.125 * jnp.dot(pair_y2, mean, precision=HI, preferred_element_type=F32)
        act_win[REACH, col, :, h * 128 : (h + 1) * 128] = mean

    def copy_a(d, to):
        return pltpu.make_async_remote_copy(
            src_ref=act_win.at[REACH, col],
            dst_ref=act_win.at[REACH - d, col],
            send_sem=sa.at[d + REACH, 0 if to is other else 1],
            recv_sem=ra.at[REACH - d, 0 if to is other else 1],
            device_id=(grp, slab + d, to),
            device_id_type=MESH,
        )

    def come_a(d, to):
        return pltpu.make_async_remote_copy(
            src_ref=act_win.at[REACH, col],
            dst_ref=act_win.at[REACH + d, to],
            send_sem=sa.at[d + REACH, 0 if to is other else 1],
            recv_sem=ra.at[REACH + d, 0 if to is other else 1],
            device_id=(grp, slab + d, to),
            device_id_type=MESH,
        )

    def each_a(act):
        for d in sorted(range(-REACH, REACH + 1), key=lambda d: -abs(d)):

            @pl.when((slab + d >= 0) & (slab + d < slabs))
            def _(d=d):
                act(d, other)
                if d != 0:
                    act(d, col)

    each_a(lambda d, to: copy_a(d, to).start())

    copy_y(0).wait_send()

    def drain(slot, c):
        both(lambda: copy_c(slot, 0).wait_send(), lambda: copy_c(slot, 1).wait_send())

        @pl.when(slot > 0)
        def _():
            copy_y(slot).wait_send()

        def tile(step, c):
            both(
                lambda: copy_z(slot, 0, step).wait_send(),
                lambda: copy_z(slot, 1, step).wait_send(),
            )
            return c

        return lax.fori_loop(0, tiles, tile, c)

    lax.fori_loop(0, SUB, drain, 0)

    def left_all(step, c):
        leave(step).wait()
        return c

    lax.fori_loop(0, tiles, left_all, 0)
    each_a(lambda d, to: copy_a(d, to).wait_send())
    each_a(lambda d, to: come_a(d, to).wait_recv())
    act_out[...] = act_win[...]


def excite(slabs, states, cond, tension):
    _, depth, rows, width = states.shape
    tiles = rows // TILE
    vmem = pl.BlockSpec(memory_space=pltpu.VMEM)
    hbm = pl.BlockSpec(memory_space=pltpu.HBM)
    window = (2 * REACH + 1, 2, *cond.shape[2:])
    dma = pltpu.SemaphoreType.DMA
    return pl.pallas_call(
        functools.partial(excite_kernel, slabs),
        out_shape=(
            jax.ShapeDtypeStruct(states.shape, F32),
            jax.ShapeDtypeStruct(tension.shape, F32),
            jax.ShapeDtypeStruct(window, F32),
        ),
        in_specs=[hbm, hbm, hbm],
        out_specs=(hbm, vmem, vmem),
        scratch_shapes=[
            pltpu.VMEM((SUB + 1, depth + 2, rows + 2 * TILE, width), F32),
            pltpu.VMEM(states.shape, F32),
            pltpu.VMEM(cond.shape, F32),
            pltpu.VMEM(tension.shape, F32),
            pltpu.VMEM((6, rows, width), F32),
            pltpu.VMEM((TILE, width), F32),
            pltpu.VMEM(window, F32),
            dma((4,)),
            dma((tiles,)),
            dma((SUB, 2, tiles)),
            dma((SUB, 2, tiles)),
            dma((SUB, 2)),
            dma((SUB, 2)),
            dma((SUB,)),
            dma((SUB,)),
            dma((2 * REACH + 1, 2)),
            dma((2 * REACH + 1, 2)),
        ],
        compiler_params=pltpu.CompilerParams(
            collective_id=0, has_side_effects=True, vmem_limit_bytes=61 << 20
        ),
        cost_estimate=pl.CostEstimate(
            flops=200_000_000, bytes_accessed=16 << 20, transcendentals=6_000_000
        ),
        name="excite",
    )(states, cond, tension)


def first_piola(f, active, fdir):
    second = {}
    for a in range(3):
        for b in range(a, 3):
            right = f[0][a] * f[0][b] + f[1][a] * f[1][b] + f[2][a] * f[2][b]
            second[a, b] = 0.5 * (right - (1.0 if a == b else 0.0))
    trace = second[0, 0] + second[1, 1] + second[2, 2]
    pull = 0.5 * active
    for a in range(3):
        scaled = pull * fdir[a]
        for b in range(a, 3):
            second[a, b] = second[a, b] + scaled * fdir[b]
        second[a, a] = second[a, a] + trace
    for a in range(3):
        for b in range(a):
            second[a, b] = second[b, a]
    return [
        f[i][0] * second[0, a] + f[i][1] * second[1, a] + f[i][2] * second[2, a]
        for a in range(3)
        for i in range(3)
    ]


def metric(f, fdir):
    cof = [[None] * 3 for _ in range(3)]
    for i in range(3):
        for j in range(3):
            cof[i][j] = (
                f[(i + 1) % 3][(j + 1) % 3] * f[(i + 2) % 3][(j + 2) % 3]
                - f[(i + 1) % 3][(j + 2) % 3] * f[(i + 2) % 3][(j + 1) % 3]
            )
    det = f[0][0] * cof[0][0] + f[0][1] * cof[0][1] + f[0][2] * cof[0][2]
    scale = 1.0 / det
    inverse = [[cof[i][j] * scale for i in range(3)] for j in range(3)]
    g = [inverse[a][0] * fdir[0] + inverse[a][1] * fdir[1] + inverse[a][2] * fdir[2] for a in range(3)]
    comps = []
    for a, b in PAIRS:
        inner = (
            inverse[a][0] * inverse[b][0]
            + inverse[a][1] * inverse[b][1]
            + inverse[a][2] * inverse[b][2]
        )
        comps.append(SIGMA_TRANS * inner + (SIGMA_LONG - SIGMA_TRANS) * (g[a] * g[b]))
    return comps


def mech_kernel(
    slabs, where, fixed, active, ten_in, states_in,
    disp_out, cond_out, ten_out, states_out, win, stress, sem,
):
    slab = where[0]
    rows, width = 2 * active.shape[2], active.shape[3]
    hand_on = pltpu.make_async_copy(states_in, states_out, sem)
    hand_on.start()
    ten_out[...] = ten_in[...]
    lane = iota2((rows, width), 1)
    line = iota2((rows, width), 0)

    def left(f):
        return jnp.where(lane == 0, 0.0, pltpu.roll(f, 1, 1))

    def right(f):
        return jnp.where(lane == width - 1, 0.0, pltpu.roll(f, width - 1, 1))

    def south(f):
        return jnp.where(line == 0, 0.0, pltpu.roll(f, 1, 0))

    def north(f):
        return jnp.where(line == rows - 1, 0.0, pltpu.roll(f, rows - 1, 0))

    def sx(f):
        return 0.125 * (left(f) + right(f)) + 0.75 * f

    def dx(f):
        return 0.5 * (right(f) - left(f))

    def sy(f):
        return 0.125 * (south(f) + north(f)) + 0.75 * f

    def dy(f):
        return 0.5 * (north(f) - south(f))

    def inside(j):
        zz = slab + j - RADIUS
        return (zz >= 0) & (zz < slabs), jnp.clip(zz, 0, slabs - 1)

    def joined(zz, n):
        return jnp.concatenate([fixed[2 * zz, n], fixed[2 * zz + 1, n]], axis=0)

    def fill(j, c):
        ok, zz = inside(j)
        for i in range(3):
            win[i, j] = jnp.where(ok, joined(zz, i), 0.0)
        return c

    lax.fori_loop(0, 2 * RADIUS + 1, fill, 0)

    def deformation(j):
        f = []
        for i in range(3):
            low, mid, high = win[i, j - 1], win[i, j], win[i, j + 1]
            zs = 0.125 * (low + high) + 0.75 * mid
            zd = 0.5 * (high - low)
            f.append([sy(sx(zd)), dy(sx(zs)), sy(dx(zs))])
            f[i][i] = f[i][i] + 1.0
        return f

    def directions(zz):
        return [joined(zz, 3 + a) for a in range(3)]

    def stresses(j, c):
        ok, zz = inside(j)
        act = jnp.concatenate([active[j - 1, 0], active[j - 1, 1]], axis=0)
        pieces = first_piola(deformation(j), act, directions(zz))
        for n in range(9):
            stress[n, j] = jnp.where(ok, pieces[n], 0.0)
        return c

    def move(j, c):
        ok, _ = inside(j)
        for i in range(3):
            zd = 0.5 * (stress[i, j + 1] - stress[i, j - 1])
            ys = 0.125 * (stress[3 + i, j - 1] + stress[3 + i, j + 1]) + 0.75 * stress[3 + i, j]
            xs = 0.125 * (stress[6 + i, j - 1] + stress[6 + i, j + 1]) + 0.75 * stress[6 + i, j]
            force = sy(sx(zd) + dx(xs)) + dy(sx(ys))
            win[i, j] = jnp.where(ok, win[i, j] + MECH_RATE * force, 0.0)
        return c

    for turn in range(MECH_STEPS):
        reach = RADIUS - 1 - 2 * turn
        lax.fori_loop(RADIUS - reach, RADIUS + reach + 1, stresses, 0)
        reach = reach - 1
        lax.fori_loop(RADIUS - reach, RADIUS + reach + 1, move, 0)

    comps = metric(deformation(RADIUS), directions(slab))
    half = disp_out.shape[2]
    first = where[1] == 0
    for i in range(3):
        whole = win[i, RADIUS]
        disp_out[i, 0] = jnp.where(first, whole[:half], whole[half:])
    for n in range(6):
        cond_out[n, 0] = jnp.where(first, comps[n][:half], comps[n][half:])
    hand_on.wait()


def mechanics(slabs, where, fixed, active, tension, states):
    _, cols, rows, width = active.shape
    full = cols * rows
    vmem = pl.BlockSpec(memory_space=pltpu.VMEM)
    hbm = pl.BlockSpec(memory_space=pltpu.HBM)
    return pl.pallas_call(
        functools.partial(mech_kernel, slabs),
        out_shape=(
            jax.ShapeDtypeStruct((3, 1, rows, width), F32),
            jax.ShapeDtypeStruct((6, 1, rows, width), F32),
            jax.ShapeDtypeStruct(tension.shape, F32),
            jax.ShapeDtypeStruct(states.shape, F32),
        ),
        in_specs=[pl.BlockSpec(memory_space=pltpu.SMEM), vmem, vmem, vmem, hbm],
        out_specs=(vmem, vmem, vmem, hbm),
        scratch_shapes=[
            pltpu.VMEM((3, 2 * RADIUS + 1, full, width), F32),
            pltpu.VMEM((9, 2 * RADIUS + 1, full, width), F32),
            pltpu.SemaphoreType.DMA,
        ],
        compiler_params=pltpu.CompilerParams(vmem_limit_bytes=61 << 20),
        name="mechanics",
    )(where, fixed, active, tension, states)


def fiber_dir(fiber):
    index = fiber.astype(F32)
    theta = -1.0 + 2.0 * index / (NFIB - 1)
    tilt = 0.3 * jnp.sin(3.0 * index)
    return jnp.stack(
        [jnp.sin(tilt), jnp.cos(tilt) * jnp.sin(theta), jnp.cos(tilt) * jnp.cos(theta)]
    )


def on_device(slabs, states, cond, tension, fiber, disp):
    fixed = jnp.concatenate([disp, fiber_dir(fiber)])
    fixed = lax.all_gather(fixed[:, 0], ("slab", "col"))
    states_next, tension_next, active = excite(slabs, states, cond, tension)
    where = jnp.stack([lax.axis_index("slab"), lax.axis_index("col")]).astype(jnp.int32)
    disp_next, cond_next, tension_next, states_next = mechanics(
        slabs, where, fixed, active, tension_next, states_next
    )
    return states_next, tension_next, disp_next, cond_next


def solution(mesh):
    wide = P(None, ("grp", "slab"), "col", None)
    flat = P(("grp", "slab"), "col", None)
    return jax.shard_map(
        functools.partial(on_device, mesh.shape["slab"]),
        mesh=mesh,
        in_specs=(wide, wide, flat, flat, wide),
        out_specs=(wide, flat, wide, wide),
        check_vma=False,
    )
```

```python
import functools

import jax
import jax.numpy as jnp
from jax import lax
from jax.experimental import pallas as pl
from jax.experimental.pallas import tpu as pltpu
from jax.sharding import PartitionSpec as P

SUB = 4
MECH_STEPS = 2
NFIB = 64
STEP_TIME = 0.05
MECH_RATE = 0.15
SIGMA_LONG = 0.16
SIGMA_TRANS = 0.04
PAIRS = ((0, 0), (1, 1), (2, 2), (0, 1), (0, 2), (1, 2))
MESH = pl.DeviceIdType.MESH
HI = lax.Precision.HIGHEST
F32 = jnp.float32
TILE = 8
CHUNK = 256
RADIUS = 2 * MECH_STEPS + 1
REACH = RADIUS - 1


def ionic(u, v, w, s):
    th_v = jnp.tanh(50.0 * (u - 0.3))
    th_w = jnp.tanh(50.0 * (u - 0.13))
    th_o = jnp.tanh(50.0 * (u - 0.006))
    th_m = jnp.tanh(65.0 * (u - 0.03))
    th_s = jnp.tanh(2.0458 * (u - 0.65))
    th_r = jnp.tanh(2.0994 * (u - 0.9087))
    hv = 0.5 + 0.5 * th_v
    hw = 0.5 + 0.5 * th_w
    ho = 0.5 + 0.5 * th_o
    nv = 1.0 - hv
    nw = 1.0 - hw
    no = 1.0 - ho
    tau_v = 605.0 + 545.0 * th_o
    tau_w = 37.5 - 22.5 * th_m
    tau_so = 15.5069 - 14.5112 * th_s
    tau_s = 9.3671 + 6.6329 * th_w
    tau_o = 203.0 - 197.0 * th_o
    w_inf = no * (1.0 - u * (1.0 / 0.07)) + 0.94 * ho
    fast = v * hv * (u - 0.3) * (1.55 - u) * (STEP_TIME / 0.11)
    slow = hw * (w * s) * (STEP_TIME / 1.8875)
    out = (u * nw * tau_so + hw * tau_o) * (STEP_TIME / (tau_o * tau_so))
    du = fast - out + slow
    inv = STEP_TIME / (tau_v * tau_w)
    v2 = v + nv * (no - v) * (tau_w * inv) - hv * v * (STEP_TIME / 1.4506)
    w2 = w + nw * (w_inf - w) * (tau_v * inv) - hw * w * (STEP_TIME / 200.0)
    s2 = s + (0.5 + 0.5 * th_r - s) * (STEP_TIME / tau_s)
    return du, v2, w2, s2


def iota2(shape, dim):
    return lax.broadcasted_iota(jnp.int32, shape, dim)


def excite_kernel(
    slabs, states, cond_hbm, ten_hbm, out_hbm, ten_out, act_out,
    ubuf, out, cond, tension, coeff, dif, act_win,
    load_sem, store_sem, sz, rz, sc, rc, sy, ry, sa, ra,
):
    grp = lax.axis_index("grp")
    slab = lax.axis_index("slab")
    col = lax.axis_index("col")
    other = 1 - col
    depth, rows, width = out.shape[1:]
    tiles = rows // TILE
    has_up = slab < slabs - 1
    has_dn = slab > 0
    edge_src = rows - (rows - TILE) * col
    edge_dst = (rows + TILE) * col

    load_u = pltpu.make_async_copy(
        states.at[0], ubuf.at[0, pl.ds(1, depth), pl.ds(TILE, rows), :], load_sem.at[0]
    )
    load_g = pltpu.make_async_copy(
        states.at[pl.ds(1, 3)], out.at[pl.ds(1, 3)], load_sem.at[1]
    )
    load_c = pltpu.make_async_copy(cond_hbm, cond, load_sem.at[2])
    load_t = pltpu.make_async_copy(ten_hbm, tension, load_sem.at[3])
    load_u.start()
    load_c.start()
    load_g.start()
    load_t.start()

    barrier = pltpu.get_barrier_semaphore()

    def greet(where):
        pl.semaphore_signal(barrier, inc=1, device_id=where, device_id_type=MESH)

    peers = -1
    for d in range(-REACH, REACH + 1):
        valid = (slab + d >= 0) & (slab + d < slabs)
        peers = peers + 2 * valid.astype(jnp.int32)

        @pl.when(valid)
        def _(d=d):
            greet((grp, slab + d, other))
            if d != 0:
                greet((grp, slab + d, col))

        @pl.when(jnp.logical_not(valid))
        def _(d=d):
            act_win[d + REACH] = jnp.zeros(act_win.shape[1:], F32)

    blank = jnp.zeros((TILE, width), F32)

    def clear_y(n, c):
        ubuf[n // (depth + 2), n % (depth + 2), pl.ds(pl.multiple_of(edge_dst, TILE), TILE), :] = blank
        return c

    lax.fori_loop(0, SUB * (depth + 2), clear_y, 0)

    def clear_z(layer):
        per = rows // TILE + 2

        def body(n, c):
            ubuf[n // per, layer, pl.ds(pl.multiple_of((n % per) * TILE, TILE), TILE), :] = blank
            return c

        lax.fori_loop(0, SUB * per, body, 0)

    @pl.when(slab == 0)
    def _():
        clear_z(0)

    @pl.when(slab == slabs - 1)
    def _():
        clear_z(depth + 1)

    def row_of(step):
        return jnp.where(col == 1, step, tiles - 1 - step)

    def copy_z(slot, way, step):
        at = pl.ds(pl.multiple_of(TILE + TILE * row_of(step), TILE), TILE)
        src = depth if way == 0 else 1
        dst = 0 if way == 0 else depth + 1
        to = slab + 1 if way == 0 else slab - 1
        return pltpu.make_async_remote_copy(
            src_ref=ubuf.at[slot, src, at, :],
            dst_ref=ubuf.at[slot, dst, at, :],
            send_sem=sz.at[slot, way, step],
            recv_sem=rz.at[slot, way, step],
            device_id=(grp, to, col),
            device_id_type=MESH,
        )

    def copy_c(slot, way):
        at = depth + 1 if way == 0 else 0
        return pltpu.make_async_remote_copy(
            src_ref=ubuf.at[slot, at, pl.ds(pl.multiple_of(edge_src, TILE), TILE), :],
            dst_ref=ubuf.at[slot, at, pl.ds(pl.multiple_of(edge_dst, TILE), TILE), :],
            send_sem=sc.at[slot, way],
            recv_sem=rc.at[slot, way],
            device_id=(grp, slab, other),
            device_id_type=MESH,
        )

    def copy_y(slot):
        return pltpu.make_async_remote_copy(
            src_ref=ubuf.at[slot, pl.ds(1, depth), pl.ds(pl.multiple_of(edge_src, TILE), TILE), :],
            dst_ref=ubuf.at[slot, pl.ds(1, depth), pl.ds(pl.multiple_of(edge_dst, TILE), TILE), :],
            send_sem=sy.at[slot],
            recv_sem=ry.at[slot],
            device_id=(grp, slab, other),
            device_id_type=MESH,
        )

    def both(do_up, do_dn):
        pl.when(has_up)(do_up)
        pl.when(has_dn)(do_dn)

    def send_z(slot, step):
        both(lambda: copy_z(slot, 0, step).start(), lambda: copy_z(slot, 1, step).start())

    def send_c(slot):
        both(lambda: copy_c(slot, 0).start(), lambda: copy_c(slot, 1).start())

    def recv_z(slot, step):
        both(lambda: copy_z(slot, 1, step).wait_recv(), lambda: copy_z(slot, 0, step).wait_recv())

    def recv_c(slot):
        both(lambda: copy_c(slot, 0).wait_recv(), lambda: copy_c(slot, 1).wait_recv())

    pl.semaphore_wait(barrier, peers)

    load_u.wait()
    send_z(0, 0)
    copy_y(0).start()

    def initial(step, c):
        send_z(0, step)
        return c

    lax.fori_loop(1, tiles, initial, 0)
    load_c.wait()

    spread_x = (iota2((128, 512), 0) == iota2((128, 512), 1) // 4).astype(F32)
    spread_y = (iota2((rows, rows // 4), 0) // 4 == iota2((rows, rows // 4), 1)).astype(F32)
    for c in range(6):
        for h in range(width // 512):
            part = jnp.dot(
                cond[c, 0, :, h * 128 : (h + 1) * 128], spread_x, precision=HI,
                preferred_element_type=F32,
            )
            part = jnp.dot(spread_y, part, precision=HI, preferred_element_type=F32)
            coeff[c, :, h * 512 : (h + 1) * 512] = part if c < 3 else 0.5 * part

    load_g.wait()
    load_t.wait()

    lane = iota2((TILE, width), 1)

    def left(f):
        return jnp.where(lane == 0, 0.0, pltpu.roll(f, 1, 1))

    def right(f):
        return jnp.where(lane == width - 1, 0.0, pltpu.roll(f, width - 1, 1))

    def layer(k, z, r):
        base = pl.multiple_of(TILE * r, TILE)
        here = pl.ds(base, TILE)
        tall = pl.ds(base, 3 * TILE)
        below = ubuf[k, z, tall, :]
        mid = ubuf[k, z + 1, tall, :]
        above = ubuf[k, z + 2, tall, :]
        odd = above - below
        centre = mid[TILE : 2 * TILE]
        odd0 = odd[TILE : 2 * TILE]
        north = mid[TILE + 1 : 2 * TILE + 1]
        south = mid[TILE - 1 : 2 * TILE - 1]
        slope = north - south
        twice = 2.0 * centre
        total = coeff[0, here, :] * (
            above[TILE : 2 * TILE] + below[TILE : 2 * TILE] - twice
        )
        total = total + coeff[1, here, :] * (north + south - twice)
        total = total + coeff[2, here, :] * (right(centre) + left(centre) - twice)
        total = total + coeff[3, here, :] * (
            odd[TILE + 1 : 2 * TILE + 1] - odd[TILE - 1 : 2 * TILE - 1]
        )
        total = total + coeff[4, here, :] * (right(odd0) - left(odd0))
        total = total + coeff[5, here, :] * (right(slope) - left(slope))
        dif[...] = total + centre
        up = pl.ds(pl.multiple_of(base + TILE, TILE), TILE)
        for x in range(0, width, CHUNK):
            xs = pl.ds(x, CHUNK)
            du, v2, w2, s2 = ionic(
                ubuf[k, z + 1, up, xs], out[1, z, here, xs], out[2, z, here, xs],
                out[3, z, here, xs],
            )
            u2 = dif[:, xs] + du
            ubuf[k + 1, z + 1, up, xs] = u2
            out[0, z, here, xs] = u2
            out[1, z, here, xs] = v2
            out[2, z, here, xs] = w2
            out[3, z, here, xs] = s2

    def leave(step):
        at = pl.ds(pl.multiple_of(TILE * row_of(step), TILE), TILE)
        return pltpu.make_async_copy(
            out.at[:, :, at, :], out_hbm.at[:, :, at, :], store_sem.at[step]
        )

    pair_x = (iota2((256, 128), 0) // 2 == iota2((256, 128), 1)).astype(F32)
    pair_y = (iota2((TILE, 2 * TILE), 0) == iota2((TILE, 2 * TILE), 1) // 2).astype(F32)
    half = rows // 2
    pair_y2 = (iota2((half // 2, half), 0) == iota2((half // 2, half), 1) // 2).astype(F32)

    def tense(p):
        fine = pl.ds(pl.multiple_of(2 * TILE * p, 2 * TILE), 2 * TILE)
        wide = pl.ds(pl.multiple_of(TILE * p, TILE), TILE)
        for q in range(depth // 2):
            layers = out[0, 2 * q, fine, :] + out[0, 2 * q + 1, fine, :]
            pairs = 0.125 * jnp.dot(pair_y, layers, precision=HI, preferred_element_type=F32)
            for h in range(width // 256):
                mean = jnp.dot(
                    pairs[:, h * 256 : (h + 1) * 256], pair_x, precision=HI,
                    preferred_element_type=F32,
                )
                xo = slice(h * 128, (h + 1) * 128)
                before = tension[q, wide, xo]
                ten_out[q, wide, xo] = before + 0.5 * (mean - before)

    def chunk(n, c):
        k = n // tiles
        step = n % tiles
        r = row_of(step)

        @pl.when(step == 0)
        def _():
            recv_z(k, 0)
            send_c(k)

        @pl.when(step < tiles - 1)
        def _():
            recv_z(k, step + 1)

        @pl.when(step == 0)
        def _():
            copy_y(k).wait_recv()
            recv_c(k)

        def outer(m, c):
            layer(k, m * (depth - 1), r)
            return c

        lax.fori_loop(0, 2, outer, 0)

        @pl.when(k < SUB - 1)
        def _():
            send_z(k + 1, step)

        def inner(m, c):
            layer(k, m, r)
            return c

        lax.fori_loop(1, depth - 1, inner, 0)

        @pl.when((k < SUB - 1) & (step == 0))
        def _():
            copy_y(k + 1).start()

        @pl.when(k == SUB - 1)
        def _():
            leave(step).start()

        @pl.when((k == SUB - 1) & (step % 2 == 1))
        def _():
            tense(r // 2)

        return c

    lax.fori_loop(0, SUB * tiles, chunk, 0)

    for h in range(width // 512):
        xs = slice(h * 256, (h + 1) * 256)
        layers = ten_out[0, :, xs] + ten_out[1, :, xs]
        mean = jnp.dot(layers, pair_x, precision=HI, preferred_element_type=F32)
        mean = 0.125 * jnp.dot(pair_y2, mean, precision=HI, preferred_element_type=F32)
        act_win[REACH, col, :, h * 128 : (h + 1) * 128] = mean

    def copy_a(d, to):
        return pltpu.make_async_remote_copy(
            src_ref=act_win.at[REACH, col],
            dst_ref=act_win.at[REACH - d, col],
            send_sem=sa.at[d + REACH, 0 if to is other else 1],
            recv_sem=ra.at[REACH - d, 0 if to is other else 1],
            device_id=(grp, slab + d, to),
            device_id_type=MESH,
        )

    def come_a(d, to):
        return pltpu.make_async_remote_copy(
            src_ref=act_win.at[REACH, col],
            dst_ref=act_win.at[REACH + d, to],
            send_sem=sa.at[d + REACH, 0 if to is other else 1],
            recv_sem=ra.at[REACH + d, 0 if to is other else 1],
            device_id=(grp, slab + d, to),
            device_id_type=MESH,
        )

    def each_a(act):
        for d in sorted(range(-REACH, REACH + 1), key=lambda d: -abs(d)):

            @pl.when((slab + d >= 0) & (slab + d < slabs))
            def _(d=d):
                act(d, other)
                if d != 0:
                    act(d, col)

    each_a(lambda d, to: copy_a(d, to).start())

    copy_y(0).wait_send()

    def drain(slot, c):
        both(lambda: copy_c(slot, 0).wait_send(), lambda: copy_c(slot, 1).wait_send())

        @pl.when(slot > 0)
        def _():
            copy_y(slot).wait_send()

        def tile(step, c):
            both(
                lambda: copy_z(slot, 0, step).wait_send(),
                lambda: copy_z(slot, 1, step).wait_send(),
            )
            return c

        return lax.fori_loop(0, tiles, tile, c)

    lax.fori_loop(0, SUB, drain, 0)

    def left_all(step, c):
        leave(step).wait()
        return c

    lax.fori_loop(0, tiles, left_all, 0)
    each_a(lambda d, to: copy_a(d, to).wait_send())
    each_a(lambda d, to: come_a(d, to).wait_recv())
    act_out[...] = act_win[...]


def excite(slabs, states, cond, tension):
    _, depth, rows, width = states.shape
    tiles = rows // TILE
    vmem = pl.BlockSpec(memory_space=pltpu.VMEM)
    hbm = pl.BlockSpec(memory_space=pltpu.HBM)
    window = (2 * REACH + 1, 2, *cond.shape[2:])
    dma = pltpu.SemaphoreType.DMA
    return pl.pallas_call(
        functools.partial(excite_kernel, slabs),
        out_shape=(
            jax.ShapeDtypeStruct(states.shape, F32),
            jax.ShapeDtypeStruct(tension.shape, F32),
            jax.ShapeDtypeStruct(window, F32),
        ),
        in_specs=[hbm, hbm, hbm],
        out_specs=(hbm, vmem, vmem),
        scratch_shapes=[
            pltpu.VMEM((SUB + 1, depth + 2, rows + 2 * TILE, width), F32),
            pltpu.VMEM(states.shape, F32),
            pltpu.VMEM(cond.shape, F32),
            pltpu.VMEM(tension.shape, F32),
            pltpu.VMEM((6, rows, width), F32),
            pltpu.VMEM((TILE, width), F32),
            pltpu.VMEM(window, F32),
            dma((4,)),
            dma((tiles,)),
            dma((SUB, 2, tiles)),
            dma((SUB, 2, tiles)),
            dma((SUB, 2)),
            dma((SUB, 2)),
            dma((SUB,)),
            dma((SUB,)),
            dma((2 * REACH + 1, 2)),
            dma((2 * REACH + 1, 2)),
        ],
        compiler_params=pltpu.CompilerParams(
            collective_id=0, has_side_effects=True, vmem_limit_bytes=61 << 20
        ),
        cost_estimate=pl.CostEstimate(
            flops=200_000_000, bytes_accessed=16 << 20, transcendentals=6_000_000
        ),
        name="excite",
    )(states, cond, tension)


def first_piola(f, active, fdir):
    second = {}
    for a in range(3):
        for b in range(a, 3):
            right = f[0][a] * f[0][b] + f[1][a] * f[1][b] + f[2][a] * f[2][b]
            second[a, b] = 0.5 * (right - (1.0 if a == b else 0.0))
    trace = second[0, 0] + second[1, 1] + second[2, 2]
    pull = 0.5 * active
    for a in range(3):
        scaled = pull * fdir[a]
        for b in range(a, 3):
            second[a, b] = second[a, b] + scaled * fdir[b]
        second[a, a] = second[a, a] + trace
    for a in range(3):
        for b in range(a):
            second[a, b] = second[b, a]
    return [
        f[i][0] * second[0, a] + f[i][1] * second[1, a] + f[i][2] * second[2, a]
        for a in range(3)
        for i in range(3)
    ]


def metric(f, fdir):
    cof = [[None] * 3 for _ in range(3)]
    for i in range(3):
        for j in range(3):
            cof[i][j] = (
                f[(i + 1) % 3][(j + 1) % 3] * f[(i + 2) % 3][(j + 2) % 3]
                - f[(i + 1) % 3][(j + 2) % 3] * f[(i + 2) % 3][(j + 1) % 3]
            )
    det = f[0][0] * cof[0][0] + f[0][1] * cof[0][1] + f[0][2] * cof[0][2]
    scale = 1.0 / det
    inverse = [[cof[i][j] * scale for i in range(3)] for j in range(3)]
    g = [inverse[a][0] * fdir[0] + inverse[a][1] * fdir[1] + inverse[a][2] * fdir[2] for a in range(3)]
    comps = []
    for a, b in PAIRS:
        inner = (
            inverse[a][0] * inverse[b][0]
            + inverse[a][1] * inverse[b][1]
            + inverse[a][2] * inverse[b][2]
        )
        comps.append(SIGMA_TRANS * inner + (SIGMA_LONG - SIGMA_TRANS) * (g[a] * g[b]))
    return comps


def mech_kernel(
    slabs, where, fixed, active, ten_in, states_in,
    disp_out, cond_out, ten_out, states_out, win, stress, held, sem,
):
    slab = where[0]
    first = where[1] == 0
    half, width = active.shape[2:]
    rows = half + TILE
    fetch = pltpu.make_async_copy(states_in, held, sem.at[0])
    hand_on = pltpu.make_async_copy(held, states_out, sem.at[1])
    fetch.start()
    ten_out[...] = ten_in[...]
    lane = iota2((rows, width), 1)
    line = iota2((rows, width), 0)

    def left(f):
        return jnp.where(lane == 0, 0.0, pltpu.roll(f, 1, 1))

    def right(f):
        return jnp.where(lane == width - 1, 0.0, pltpu.roll(f, width - 1, 1))

    def south(f):
        return jnp.where(line == 0, 0.0, pltpu.roll(f, 1, 0))

    def north(f):
        return jnp.where(line == rows - 1, 0.0, pltpu.roll(f, rows - 1, 0))

    def sx(f):
        return 0.125 * (left(f) + right(f)) + 0.75 * f

    def dx(f):
        return 0.5 * (right(f) - left(f))

    def sy(f):
        return 0.125 * (south(f) + north(f)) + 0.75 * f

    def dy(f):
        return 0.5 * (north(f) - south(f))

    def inside(j):
        zz = slab + j - RADIUS
        return (zz >= 0) & (zz < slabs), jnp.clip(zz, 0, slabs - 1)

    def beside(a, b):
        return jnp.where(
            first,
            jnp.concatenate([a, b[:TILE]], axis=0),
            jnp.concatenate([a[half - TILE :], b], axis=0),
        )

    def joined(zz, n):
        return beside(fixed[2 * zz, n], fixed[2 * zz + 1, n])

    def fill(j, c):
        ok, zz = inside(j)
        for i in range(3):
            win[i, j] = jnp.where(ok, joined(zz, i), 0.0)
        return c

    lax.fori_loop(0, 2 * RADIUS + 1, fill, 0)

    def deformation(j):
        f = []
        for i in range(3):
            low, mid, high = win[i, j - 1], win[i, j], win[i, j + 1]
            zs = 0.125 * (low + high) + 0.75 * mid
            zd = 0.5 * (high - low)
            f.append([sy(sx(zd)), dy(sx(zs)), sy(dx(zs))])
            f[i][i] = f[i][i] + 1.0
        return f

    def directions(zz):
        return [joined(zz, 3 + a) for a in range(3)]

    def stresses(j, c):
        ok, zz = inside(j)
        act = beside(active[j - 1, 0], active[j - 1, 1])
        pieces = first_piola(deformation(j), act, directions(zz))
        for n in range(9):
            stress[n, j] = jnp.where(ok, pieces[n], 0.0)
        return c

    def move(j, c):
        ok, _ = inside(j)
        for i in range(3):
            zd = 0.5 * (stress[i, j + 1] - stress[i, j - 1])
            ys = 0.125 * (stress[3 + i, j - 1] + stress[3 + i, j + 1]) + 0.75 * stress[3 + i, j]
            xs = 0.125 * (stress[6 + i, j - 1] + stress[6 + i, j + 1]) + 0.75 * stress[6 + i, j]
            force = sy(sx(zd) + dx(xs)) + dy(sx(ys))
            win[i, j] = jnp.where(ok, win[i, j] + MECH_RATE * force, 0.0)
        return c

    for turn in range(MECH_STEPS):
        reach = RADIUS - 1 - 2 * turn
        lax.fori_loop(RADIUS - reach, RADIUS + reach + 1, stresses, 0)
        if turn == 0:
            fetch.wait()
            hand_on.start()
        reach = reach - 1
        lax.fori_loop(RADIUS - reach, RADIUS + reach + 1, move, 0)

    comps = metric(deformation(RADIUS), directions(slab))
    for i in range(3):
        whole = win[i, RADIUS]
        disp_out[i, 0] = jnp.where(first, whole[:half], whole[TILE:])
    for n in range(6):
        cond_out[n, 0] = jnp.where(first, comps[n][:half], comps[n][TILE:])
    hand_on.wait()


def mechanics(slabs, where, fixed, active, tension, states):
    _, _, rows, width = active.shape
    full = rows + TILE
    vmem = pl.BlockSpec(memory_space=pltpu.VMEM)
    hbm = pl.BlockSpec(memory_space=pltpu.HBM)
    return pl.pallas_call(
        functools.partial(mech_kernel, slabs),
        out_shape=(
            jax.ShapeDtypeStruct((3, 1, rows, width), F32),
            jax.ShapeDtypeStruct((6, 1, rows, width), F32),
            jax.ShapeDtypeStruct(tension.shape, F32),
            jax.ShapeDtypeStruct(states.shape, F32),
        ),
        in_specs=[pl.BlockSpec(memory_space=pltpu.SMEM), vmem, vmem, vmem, hbm],
        out_specs=(vmem, vmem, vmem, hbm),
        scratch_shapes=[
            pltpu.VMEM((3, 2 * RADIUS + 1, full, width), F32),
            pltpu.VMEM((9, 2 * RADIUS + 1, full, width), F32),
            pltpu.VMEM(states.shape, F32),
            pltpu.SemaphoreType.DMA((2,)),
        ],
        compiler_params=pltpu.CompilerParams(vmem_limit_bytes=61 << 20),
        name="mechanics",
    )(where, fixed, active, tension, states)


def fiber_dir(fiber):
    index = fiber.astype(F32)
    theta = -1.0 + 2.0 * index / (NFIB - 1)
    tilt = 0.3 * jnp.sin(3.0 * index)
    return jnp.stack(
        [jnp.sin(tilt), jnp.cos(tilt) * jnp.sin(theta), jnp.cos(tilt) * jnp.cos(theta)]
    )


def on_device(slabs, states, cond, tension, fiber, disp):
    fixed = jnp.concatenate([disp, fiber_dir(fiber)])
    fixed = lax.all_gather(fixed[:, 0], ("slab", "col"))
    states_next, tension_next, active = excite(slabs, states, cond, tension)
    where = jnp.stack([lax.axis_index("slab"), lax.axis_index("col")]).astype(jnp.int32)
    disp_next, cond_next, tension_next, states_next = mechanics(
        slabs, where, fixed, active, tension_next, states_next
    )
    return states_next, tension_next, disp_next, cond_next


def solution(mesh):
    wide = P(None, ("grp", "slab"), "col", None)
    flat = P(("grp", "slab"), "col", None)
    return jax.shard_map(
        functools.partial(on_device, mesh.shape["slab"]),
        mesh=mesh,
        in_specs=(wide, wide, flat, flat, wide),
        out_specs=(wide, flat, wide, wide),
        check_vma=False,
    )
```

```python
import functools

import jax
import jax.numpy as jnp
from jax import lax
from jax.experimental import pallas as pl
from jax.experimental.pallas import tpu as pltpu
from jax.sharding import PartitionSpec as P

SUB = 4
MECH_STEPS = 2
NFIB = 64
STEP_TIME = 0.05
MECH_RATE = 0.15
SIGMA_LONG = 0.16
SIGMA_TRANS = 0.04
PAIRS = ((0, 0), (1, 1), (2, 2), (0, 1), (0, 2), (1, 2))
MESH = pl.DeviceIdType.MESH
HI = lax.Precision.HIGHEST
F32 = jnp.float32
TILE = 8
CHUNK = 256
RADIUS = 2 * MECH_STEPS + 1
REACH = RADIUS - 1


def ionic(u, v, w, s):
    th_v = jnp.tanh(50.0 * (u - 0.3))
    th_w = jnp.tanh(50.0 * (u - 0.13))
    th_o = jnp.tanh(50.0 * (u - 0.006))
    th_m = jnp.tanh(65.0 * (u - 0.03))
    th_s = jnp.tanh(2.0458 * (u - 0.65))
    th_r = jnp.tanh(2.0994 * (u - 0.9087))
    hv = 0.5 + 0.5 * th_v
    hw = 0.5 + 0.5 * th_w
    ho = 0.5 + 0.5 * th_o
    nv = 1.0 - hv
    nw = 1.0 - hw
    no = 1.0 - ho
    tau_v = 605.0 + 545.0 * th_o
    tau_w = 37.5 - 22.5 * th_m
    tau_so = 15.5069 - 14.5112 * th_s
    tau_s = 9.3671 + 6.6329 * th_w
    tau_o = 203.0 - 197.0 * th_o
    w_inf = no * (1.0 - u * (1.0 / 0.07)) + 0.94 * ho
    fast = v * hv * (u - 0.3) * (1.55 - u) * (STEP_TIME / 0.11)
    slow = hw * (w * s) * (STEP_TIME / 1.8875)
    out = (u * nw * tau_so + hw * tau_o) * (STEP_TIME / (tau_o * tau_so))
    du = fast - out + slow
    inv = STEP_TIME / (tau_v * tau_w)
    v2 = v + nv * (no - v) * (tau_w * inv) - hv * v * (STEP_TIME / 1.4506)
    w2 = w + nw * (w_inf - w) * (tau_v * inv) - hw * w * (STEP_TIME / 200.0)
    s2 = s + (0.5 + 0.5 * th_r - s) * (STEP_TIME / tau_s)
    return du, v2, w2, s2


def iota2(shape, dim):
    return lax.broadcasted_iota(jnp.int32, shape, dim)


def excite_kernel(
    slabs, states, cond_hbm, ten_hbm, fix_hbm, out_hbm, ten_out, act_out, fix_out,
    ubuf, out, cond, tension, coeff, dif, act_win,
    fix_win, load_sem, store_sem, sz, rz, sc, rc, sy, ry, sa, ra, sf, rf,
):
    grp = lax.axis_index("grp")
    slab = lax.axis_index("slab")
    col = lax.axis_index("col")
    other = 1 - col
    depth, rows, width = out.shape[1:]
    tiles = rows // TILE
    has_up = slab < slabs - 1
    has_dn = slab > 0
    edge_src = rows - (rows - TILE) * col
    edge_dst = (rows + TILE) * col

    load_u = pltpu.make_async_copy(
        states.at[0], ubuf.at[0, pl.ds(1, depth), pl.ds(TILE, rows), :], load_sem.at[0]
    )
    load_g = pltpu.make_async_copy(
        states.at[pl.ds(1, 3)], out.at[pl.ds(1, 3)], load_sem.at[1]
    )
    load_c = pltpu.make_async_copy(cond_hbm, cond, load_sem.at[2])
    load_t = pltpu.make_async_copy(ten_hbm, tension, load_sem.at[3])
    load_u.start()
    load_c.start()
    load_g.start()
    load_t.start()
    load_f = pltpu.make_async_copy(fix_hbm, fix_win.at[RADIUS, col], load_sem.at[4])
    load_f.start()

    barrier = pltpu.get_barrier_semaphore()

    def greet(where):
        pl.semaphore_signal(barrier, inc=1, device_id=where, device_id_type=MESH)

    peers = -1
    for d in range(-RADIUS, RADIUS + 1):
        valid = (slab + d >= 0) & (slab + d < slabs)
        peers = peers + 2 * valid.astype(jnp.int32)

        @pl.when(valid)
        def _(d=d):
            greet((grp, slab + d, other))
            if d != 0:
                greet((grp, slab + d, col))

        @pl.when(jnp.logical_not(valid))
        def _(d=d):
            fix_win[d + RADIUS, col] = jnp.zeros(fix_win.shape[2:], F32)
            if abs(d) <= REACH:
                act_win[d + REACH] = jnp.zeros(act_win.shape[1:], F32)

    blank = jnp.zeros((TILE, width), F32)

    def clear_y(n, c):
        ubuf[n // (depth + 2), n % (depth + 2), pl.ds(pl.multiple_of(edge_dst, TILE), TILE), :] = blank
        return c

    lax.fori_loop(0, SUB * (depth + 2), clear_y, 0)

    def clear_z(layer):
        per = rows // TILE + 2

        def body(n, c):
            ubuf[n // per, layer, pl.ds(pl.multiple_of((n % per) * TILE, TILE), TILE), :] = blank
            return c

        lax.fori_loop(0, SUB * per, body, 0)

    @pl.when(slab == 0)
    def _():
        clear_z(0)

    @pl.when(slab == slabs - 1)
    def _():
        clear_z(depth + 1)

    def row_of(step):
        return jnp.where(col == 1, step, tiles - 1 - step)

    def copy_z(slot, way, step):
        at = pl.ds(pl.multiple_of(TILE + TILE * row_of(step), TILE), TILE)
        src = depth if way == 0 else 1
        dst = 0 if way == 0 else depth + 1
        to = slab + 1 if way == 0 else slab - 1
        return pltpu.make_async_remote_copy(
            src_ref=ubuf.at[slot, src, at, :],
            dst_ref=ubuf.at[slot, dst, at, :],
            send_sem=sz.at[slot, way, step],
            recv_sem=rz.at[slot, way, step],
            device_id=(grp, to, col),
            device_id_type=MESH,
        )

    def copy_c(slot, way):
        at = depth + 1 if way == 0 else 0
        return pltpu.make_async_remote_copy(
            src_ref=ubuf.at[slot, at, pl.ds(pl.multiple_of(edge_src, TILE), TILE), :],
            dst_ref=ubuf.at[slot, at, pl.ds(pl.multiple_of(edge_dst, TILE), TILE), :],
            send_sem=sc.at[slot, way],
            recv_sem=rc.at[slot, way],
            device_id=(grp, slab, other),
            device_id_type=MESH,
        )

    def copy_y(slot):
        return pltpu.make_async_remote_copy(
            src_ref=ubuf.at[slot, pl.ds(1, depth), pl.ds(pl.multiple_of(edge_src, TILE), TILE), :],
            dst_ref=ubuf.at[slot, pl.ds(1, depth), pl.ds(pl.multiple_of(edge_dst, TILE), TILE), :],
            send_sem=sy.at[slot],
            recv_sem=ry.at[slot],
            device_id=(grp, slab, other),
            device_id_type=MESH,
        )

    def both(do_up, do_dn):
        pl.when(has_up)(do_up)
        pl.when(has_dn)(do_dn)

    def send_z(slot, step):
        both(lambda: copy_z(slot, 0, step).start(), lambda: copy_z(slot, 1, step).start())

    def send_c(slot):
        both(lambda: copy_c(slot, 0).start(), lambda: copy_c(slot, 1).start())

    def recv_z(slot, step):
        both(lambda: copy_z(slot, 1, step).wait_recv(), lambda: copy_z(slot, 0, step).wait_recv())

    def recv_c(slot):
        both(lambda: copy_c(slot, 0).wait_recv(), lambda: copy_c(slot, 1).wait_recv())

    pl.semaphore_wait(barrier, peers)

    load_u.wait()
    send_z(0, 0)
    copy_y(0).start()

    def initial(step, c):
        send_z(0, step)
        return c

    lax.fori_loop(1, tiles, initial, 0)
    load_c.wait()

    spread_x = (iota2((128, 512), 0) == iota2((128, 512), 1) // 4).astype(F32)
    spread_y = (iota2((rows, rows // 4), 0) // 4 == iota2((rows, rows // 4), 1)).astype(F32)
    for c in range(6):
        for h in range(width // 512):
            part = jnp.dot(
                cond[c, 0, :, h * 128 : (h + 1) * 128], spread_x, precision=HI,
                preferred_element_type=F32,
            )
            part = jnp.dot(spread_y, part, precision=HI, preferred_element_type=F32)
            coeff[c, :, h * 512 : (h + 1) * 512] = part if c < 3 else 0.5 * part

    load_g.wait()
    load_t.wait()

    def copy_f(d):
        return pltpu.make_async_remote_copy(
            src_ref=fix_win.at[RADIUS, col],
            dst_ref=fix_win.at[RADIUS - d, col],
            send_sem=sf.at[d + RADIUS],
            recv_sem=rf.at[RADIUS - d],
            device_id=(grp, slab + d, col),
            device_id_type=MESH,
        )

    def come_f(d):
        return pltpu.make_async_remote_copy(
            src_ref=fix_win.at[RADIUS, col],
            dst_ref=fix_win.at[RADIUS + d, col],
            send_sem=sf.at[d + RADIUS],
            recv_sem=rf.at[RADIUS + d],
            device_id=(grp, slab + d, col),
            device_id_type=MESH,
        )

    def share_f(whose):
        return pltpu.make_async_remote_copy(
            src_ref=fix_win.at[:, whose],
            dst_ref=fix_win.at[:, whose],
            send_sem=sf.at[RADIUS],
            recv_sem=rf.at[RADIUS],
            device_id=(grp, slab, other),
            device_id_type=MESH,
        )

    def each_f(act):
        for d in range(-RADIUS, RADIUS + 1):
            if d != 0:
                pl.when((slab + d >= 0) & (slab + d < slabs))(lambda d=d: act(d))

    load_f.wait()
    each_f(lambda d: copy_f(d).start())

    lane = iota2((TILE, width), 1)

    def left(f):
        return jnp.where(lane == 0, 0.0, pltpu.roll(f, 1, 1))

    def right(f):
        return jnp.where(lane == width - 1, 0.0, pltpu.roll(f, width - 1, 1))

    def layer(k, z, r):
        base = pl.multiple_of(TILE * r, TILE)
        here = pl.ds(base, TILE)
        tall = pl.ds(base, 3 * TILE)
        below = ubuf[k, z, tall, :]
        mid = ubuf[k, z + 1, tall, :]
        above = ubuf[k, z + 2, tall, :]
        odd = above - below
        centre = mid[TILE : 2 * TILE]
        odd0 = odd[TILE : 2 * TILE]
        north = mid[TILE + 1 : 2 * TILE + 1]
        south = mid[TILE - 1 : 2 * TILE - 1]
        slope = north - south
        twice = 2.0 * centre
        total = coeff[0, here, :] * (
            above[TILE : 2 * TILE] + below[TILE : 2 * TILE] - twice
        )
        total = total + coeff[1, here, :] * (north + south - twice)
        total = total + coeff[2, here, :] * (right(centre) + left(centre) - twice)
        total = total + coeff[3, here, :] * (
            odd[TILE + 1 : 2 * TILE + 1] - odd[TILE - 1 : 2 * TILE - 1]
        )
        total = total + coeff[4, here, :] * (right(odd0) - left(odd0))
        total = total + coeff[5, here, :] * (right(slope) - left(slope))
        dif[...] = total + centre
        up = pl.ds(pl.multiple_of(base + TILE, TILE), TILE)
        for x in range(0, width, CHUNK):
            xs = pl.ds(x, CHUNK)
            du, v2, w2, s2 = ionic(
                ubuf[k, z + 1, up, xs], out[1, z, here, xs], out[2, z, here, xs],
                out[3, z, here, xs],
            )
            u2 = dif[:, xs] + du
            ubuf[k + 1, z + 1, up, xs] = u2
            out[0, z, here, xs] = u2
            out[1, z, here, xs] = v2
            out[2, z, here, xs] = w2
            out[3, z, here, xs] = s2

    def leave(step):
        at = pl.ds(pl.multiple_of(TILE * row_of(step), TILE), TILE)
        return pltpu.make_async_copy(
            out.at[:, :, at, :], out_hbm.at[:, :, at, :], store_sem.at[step]
        )

    pair_x = (iota2((256, 128), 0) // 2 == iota2((256, 128), 1)).astype(F32)
    pair_y = (iota2((TILE, 2 * TILE), 0) == iota2((TILE, 2 * TILE), 1) // 2).astype(F32)
    half = rows // 2
    pair_y2 = (iota2((half // 2, half), 0) == iota2((half // 2, half), 1) // 2).astype(F32)

    def tense(p):
        fine = pl.ds(pl.multiple_of(2 * TILE * p, 2 * TILE), 2 * TILE)
        wide = pl.ds(pl.multiple_of(TILE * p, TILE), TILE)
        for q in range(depth // 2):
            layers = out[0, 2 * q, fine, :] + out[0, 2 * q + 1, fine, :]
            pairs = 0.125 * jnp.dot(pair_y, layers, precision=HI, preferred_element_type=F32)
            for h in range(width // 256):
                mean = jnp.dot(
                    pairs[:, h * 256 : (h + 1) * 256], pair_x, precision=HI,
                    preferred_element_type=F32,
                )
                xo = slice(h * 128, (h + 1) * 128)
                before = tension[q, wide, xo]
                ten_out[q, wide, xo] = before + 0.5 * (mean - before)

    def chunk(n, c):
        k = n // tiles
        step = n % tiles
        r = row_of(step)

        @pl.when(n == 2 * tiles)
        def _():
            each_f(lambda d: come_f(d).wait_recv())
            share_f(col).start()

        @pl.when(step == 0)
        def _():
            recv_z(k, 0)
            send_c(k)

        @pl.when(step < tiles - 1)
        def _():
            recv_z(k, step + 1)

        @pl.when(step == 0)
        def _():
            copy_y(k).wait_recv()
            recv_c(k)

        def outer(m, c):
            layer(k, m * (depth - 1), r)
            return c

        lax.fori_loop(0, 2, outer, 0)

        @pl.when(k < SUB - 1)
        def _():
            send_z(k + 1, step)

        def inner(m, c):
            layer(k, m, r)
            return c

        lax.fori_loop(1, depth - 1, inner, 0)

        @pl.when((k < SUB - 1) & (step == 0))
        def _():
            copy_y(k + 1).start()

        @pl.when(k == SUB - 1)
        def _():
            leave(step).start()

        @pl.when((k == SUB - 1) & (step % 2 == 1))
        def _():
            tense(r // 2)

        return c

    lax.fori_loop(0, SUB * tiles, chunk, 0)

    for h in range(width // 512):
        xs = slice(h * 256, (h + 1) * 256)
        layers = ten_out[0, :, xs] + ten_out[1, :, xs]
        mean = jnp.dot(layers, pair_x, precision=HI, preferred_element_type=F32)
        mean = 0.125 * jnp.dot(pair_y2, mean, precision=HI, preferred_element_type=F32)
        act_win[REACH, col, :, h * 128 : (h + 1) * 128] = mean

    def copy_a(d, to):
        return pltpu.make_async_remote_copy(
            src_ref=act_win.at[REACH, col],
            dst_ref=act_win.at[REACH - d, col],
            send_sem=sa.at[d + REACH, 0 if to is other else 1],
            recv_sem=ra.at[REACH - d, 0 if to is other else 1],
            device_id=(grp, slab + d, to),
            device_id_type=MESH,
        )

    def come_a(d, to):
        return pltpu.make_async_remote_copy(
            src_ref=act_win.at[REACH, col],
            dst_ref=act_win.at[REACH + d, to],
            send_sem=sa.at[d + REACH, 0 if to is other else 1],
            recv_sem=ra.at[REACH + d, 0 if to is other else 1],
            device_id=(grp, slab + d, to),
            device_id_type=MESH,
        )

    def each_a(act):
        for d in sorted(range(-REACH, REACH + 1), key=lambda d: -abs(d)):

            @pl.when((slab + d >= 0) & (slab + d < slabs))
            def _(d=d):
                act(d, other)
                if d != 0:
                    act(d, col)

    each_a(lambda d, to: copy_a(d, to).start())
    share_f(col).wait_send()
    share_f(other).wait_recv()
    each_f(lambda d: copy_f(d).wait_send())

    def show(j, c):
        fix_out[j] = fix_win[j]
        return c

    lax.fori_loop(0, 2 * RADIUS + 1, show, 0)

    copy_y(0).wait_send()

    def drain(slot, c):
        both(lambda: copy_c(slot, 0).wait_send(), lambda: copy_c(slot, 1).wait_send())

        @pl.when(slot > 0)
        def _():
            copy_y(slot).wait_send()

        def tile(step, c):
            both(
                lambda: copy_z(slot, 0, step).wait_send(),
                lambda: copy_z(slot, 1, step).wait_send(),
            )
            return c

        return lax.fori_loop(0, tiles, tile, c)

    lax.fori_loop(0, SUB, drain, 0)

    def left_all(step, c):
        leave(step).wait()
        return c

    lax.fori_loop(0, tiles, left_all, 0)
    each_a(lambda d, to: copy_a(d, to).wait_send())
    each_a(lambda d, to: come_a(d, to).wait_recv())
    act_out[...] = act_win[...]


def excite(slabs, states, cond, tension, fixed):
    _, depth, rows, width = states.shape
    tiles = rows // TILE
    vmem = pl.BlockSpec(memory_space=pltpu.VMEM)
    hbm = pl.BlockSpec(memory_space=pltpu.HBM)
    window = (2 * REACH + 1, 2, *cond.shape[2:])
    broad = (2 * RADIUS + 1, 2, *fixed.shape)
    dma = pltpu.SemaphoreType.DMA
    return pl.pallas_call(
        functools.partial(excite_kernel, slabs),
        out_shape=(
            jax.ShapeDtypeStruct(states.shape, F32),
            jax.ShapeDtypeStruct(tension.shape, F32),
            jax.ShapeDtypeStruct(window, F32),
            jax.ShapeDtypeStruct(broad, F32),
        ),
        in_specs=[hbm, hbm, hbm, hbm],
        out_specs=(hbm, vmem, vmem, vmem),
        scratch_shapes=[
            pltpu.VMEM((SUB + 1, depth + 2, rows + 2 * TILE, width), F32),
            pltpu.VMEM(states.shape, F32),
            pltpu.VMEM(cond.shape, F32),
            pltpu.VMEM(tension.shape, F32),
            pltpu.VMEM((6, rows, width), F32),
            pltpu.VMEM((TILE, width), F32),
            pltpu.VMEM(window, F32),
            pltpu.VMEM(broad, F32),
            dma((5,)),
            dma((tiles,)),
            dma((SUB, 2, tiles)),
            dma((SUB, 2, tiles)),
            dma((SUB, 2)),
            dma((SUB, 2)),
            dma((SUB,)),
            dma((SUB,)),
            dma((2 * REACH + 1, 2)),
            dma((2 * REACH + 1, 2)),
            dma((2 * RADIUS + 1,)),
            dma((2 * RADIUS + 1,)),
        ],
        compiler_params=pltpu.CompilerParams(
            collective_id=0, has_side_effects=True, vmem_limit_bytes=61 << 20
        ),
        cost_estimate=pl.CostEstimate(
            flops=200_000_000, bytes_accessed=16 << 20, transcendentals=6_000_000
        ),
        name="excite",
    )(states, cond, tension, fixed)


def first_piola(f, active, fdir):
    second = {}
    for a in range(3):
        for b in range(a, 3):
            right = f[0][a] * f[0][b] + f[1][a] * f[1][b] + f[2][a] * f[2][b]
            second[a, b] = 0.5 * (right - (1.0 if a == b else 0.0))
    trace = second[0, 0] + second[1, 1] + second[2, 2]
    pull = 0.5 * active
    for a in range(3):
        scaled = pull * fdir[a]
        for b in range(a, 3):
            second[a, b] = second[a, b] + scaled * fdir[b]
        second[a, a] = second[a, a] + trace
    for a in range(3):
        for b in range(a):
            second[a, b] = second[b, a]
    return [
        f[i][0] * second[0, a] + f[i][1] * second[1, a] + f[i][2] * second[2, a]
        for a in range(3)
        for i in range(3)
    ]


def metric(f, fdir):
    cof = [[None] * 3 for _ in range(3)]
    for i in range(3):
        for j in range(3):
            cof[i][j] = (
                f[(i + 1) % 3][(j + 1) % 3] * f[(i + 2) % 3][(j + 2) % 3]
                - f[(i + 1) % 3][(j + 2) % 3] * f[(i + 2) % 3][(j + 1) % 3]
            )
    det = f[0][0] * cof[0][0] + f[0][1] * cof[0][1] + f[0][2] * cof[0][2]
    scale = 1.0 / det
    inverse = [[cof[i][j] * scale for i in range(3)] for j in range(3)]
    g = [inverse[a][0] * fdir[0] + inverse[a][1] * fdir[1] + inverse[a][2] * fdir[2] for a in range(3)]
    comps = []
    for a, b in PAIRS:
        inner = (
            inverse[a][0] * inverse[b][0]
            + inverse[a][1] * inverse[b][1]
            + inverse[a][2] * inverse[b][2]
        )
        comps.append(SIGMA_TRANS * inner + (SIGMA_LONG - SIGMA_TRANS) * (g[a] * g[b]))
    return comps


def mech_kernel(
    slabs, where, fixed, active, ten_in, states_in,
    disp_out, cond_out, ten_out, states_out, win, stress, held, sem,
):
    slab = where[0]
    first = where[1] == 0
    half, width = active.shape[2:]
    rows = half + TILE
    fetch = pltpu.make_async_copy(states_in, held, sem.at[0])
    hand_on = pltpu.make_async_copy(held, states_out, sem.at[1])
    fetch.start()
    ten_out[...] = ten_in[...]
    lane = iota2((rows, width), 1)
    line = iota2((rows, width), 0)

    def left(f):
        return jnp.where(lane == 0, 0.0, pltpu.roll(f, 1, 1))

    def right(f):
        return jnp.where(lane == width - 1, 0.0, pltpu.roll(f, width - 1, 1))

    def south(f):
        return jnp.where(line == 0, 0.0, pltpu.roll(f, 1, 0))

    def north(f):
        return jnp.where(line == rows - 1, 0.0, pltpu.roll(f, rows - 1, 0))

    def sx(f):
        return 0.125 * (left(f) + right(f)) + 0.75 * f

    def dx(f):
        return 0.5 * (right(f) - left(f))

    def sy(f):
        return 0.125 * (south(f) + north(f)) + 0.75 * f

    def dy(f):
        return 0.5 * (north(f) - south(f))

    def inside(j):
        zz = slab + j - RADIUS
        return (zz >= 0) & (zz < slabs), jnp.clip(zz, 0, slabs - 1)

    def beside(a, b):
        return jnp.where(
            first,
            jnp.concatenate([a, b[:TILE]], axis=0),
            jnp.concatenate([a[half - TILE :], b], axis=0),
        )

    def joined(j, n):
        return beside(fixed[j, 0, n], fixed[j, 1, n])

    def fill(j, c):
        ok, zz = inside(j)
        for i in range(3):
            win[i, j] = jnp.where(ok, joined(j, i), 0.0)
        return c

    lax.fori_loop(0, 2 * RADIUS + 1, fill, 0)

    def deformation(j):
        f = []
        for i in range(3):
            low, mid, high = win[i, j - 1], win[i, j], win[i, j + 1]
            zs = 0.125 * (low + high) + 0.75 * mid
            zd = 0.5 * (high - low)
            f.append([sy(sx(zd)), dy(sx(zs)), sy(dx(zs))])
            f[i][i] = f[i][i] + 1.0
        return f

    def sine(x):
        y = x * x
        c = 1.0
        for n in (12, 10, 8, 6, 4, 2):
            c = 1.0 - y * (1.0 / (n * (n + 1))) * c
        return x * c

    def cosine(x):
        y = x * x
        c = 1.0
        for n in (13, 11, 9, 7, 5, 3, 1):
            c = 1.0 - y * (1.0 / (n * (n + 1))) * c
        return c

    def directions(j):
        index = joined(j, 3)
        theta = -1.0 + index * (2.0 / (NFIB - 1))
        tilt = 0.3 * jnp.sin(3.0 * index)
        flat = cosine(tilt)
        return [sine(tilt), flat * sine(theta), flat * cosine(theta)]

    def stresses(j, c):
        ok, zz = inside(j)
        act = beside(active[j - 1, 0], active[j - 1, 1])
        pieces = first_piola(deformation(j), act, directions(j))
        for n in range(9):
            stress[n, j] = jnp.where(ok, pieces[n], 0.0)
        return c

    def move(j, c):
        ok, _ = inside(j)
        for i in range(3):
            zd = 0.5 * (stress[i, j + 1] - stress[i, j - 1])
            ys = 0.125 * (stress[3 + i, j - 1] + stress[3 + i, j + 1]) + 0.75 * stress[3 + i, j]
            xs = 0.125 * (stress[6 + i, j - 1] + stress[6 + i, j + 1]) + 0.75 * stress[6 + i, j]
            force = sy(sx(zd) + dx(xs)) + dy(sx(ys))
            win[i, j] = jnp.where(ok, win[i, j] + MECH_RATE * force, 0.0)
        return c

    for turn in range(MECH_STEPS):
        reach = RADIUS - 1 - 2 * turn
        lax.fori_loop(RADIUS - reach, RADIUS + reach + 1, stresses, 0)
        if turn == 0:
            fetch.wait()
            hand_on.start()
        reach = reach - 1
        lax.fori_loop(RADIUS - reach, RADIUS + reach + 1, move, 0)

    comps = metric(deformation(RADIUS), directions(RADIUS))
    for i in range(3):
        whole = win[i, RADIUS]
        disp_out[i, 0] = jnp.where(first, whole[:half], whole[TILE:])
    for n in range(6):
        cond_out[n, 0] = jnp.where(first, comps[n][:half], comps[n][TILE:])
    hand_on.wait()


def mechanics(slabs, where, fixed, active, tension, states):
    _, _, rows, width = active.shape
    full = rows + TILE
    vmem = pl.BlockSpec(memory_space=pltpu.VMEM)
    hbm = pl.BlockSpec(memory_space=pltpu.HBM)
    return pl.pallas_call(
        functools.partial(mech_kernel, slabs),
        out_shape=(
            jax.ShapeDtypeStruct((3, 1, rows, width), F32),
            jax.ShapeDtypeStruct((6, 1, rows, width), F32),
            jax.ShapeDtypeStruct(tension.shape, F32),
            jax.ShapeDtypeStruct(states.shape, F32),
        ),
        in_specs=[pl.BlockSpec(memory_space=pltpu.SMEM), vmem, vmem, vmem, hbm],
        out_specs=(vmem, vmem, vmem, hbm),
        scratch_shapes=[
            pltpu.VMEM((3, 2 * RADIUS + 1, full, width), F32),
            pltpu.VMEM((9, 2 * RADIUS + 1, full, width), F32),
            pltpu.VMEM(states.shape, F32),
            pltpu.SemaphoreType.DMA((2,)),
        ],
        compiler_params=pltpu.CompilerParams(vmem_limit_bytes=61 << 20),
        name="mechanics",
    )(where, fixed, active, tension, states)


def on_device(slabs, states, cond, tension, fiber, disp):
    fixed = jnp.concatenate([disp[:, 0], fiber.astype(F32)])
    states_next, tension_next, active, fixed = excite(slabs, states, cond, tension, fixed)
    where = jnp.stack([lax.axis_index("slab"), lax.axis_index("col")]).astype(jnp.int32)
    disp_next, cond_next, tension_next, states_next = mechanics(
        slabs, where, fixed, active, tension_next, states_next
    )
    return states_next, tension_next, disp_next, cond_next


def solution(mesh):
    wide = P(None, ("grp", "slab"), "col", None)
    flat = P(("grp", "slab"), "col", None)
    return jax.shard_map(
        functools.partial(on_device, mesh.shape["slab"]),
        mesh=mesh,
        in_specs=(wide, wide, flat, flat, wide),
        out_specs=(wide, flat, wide, wide),
        check_vma=False,
    )
```
